32 devices in a mesh: tile: 8 (over z, y), mode: 4 (over x, core).
Axes of the slice: x: 2, y: 2, z: 4, core: 2. Of those that a mesh axis runs over, the one named last changes fastest.
Arguments:
- cycle_spectra: float32 [2, 4096, 16, 256], P(None, 'mode', 'tile'), may hold values from -6 to 6
- link_phase: int32 [2, 16, 256], P(None, 'tile'), may hold values from 0 to 63
- pump_mask: int32 [16, 256], P('tile'), may hold values 0 or 1
- detuning: float32 [16, 256], P('tile'), may hold values from -1 to 1
Outputs:
- cycle_samples: float32 [2, 4096, 16, 256], P(None, 'mode', 'tile')
The draws below stay inside these ranges and needn't reach their ends.
All inputs are finite; a program needn't handle non-finite values. No bound on the sum of `pump_mask` on one device may be relied on, other than what follows from the above.
Results may differ from the reference program's by a relative error of at most 0.0003.
Values sent between devices are 32-bit elements; how exact they have to be, the bound alone decides.
A program may use at most 128 MiB of HBM per device.

```python
import math
import jax
import jax.numpy as jnp
from jax import lax

FACTOR = 64
M = 4096
NY = 256
NX = 16
ROUNDS = 2


def place_ends(result, rng, low, top_value):
    shape = result.shape
    place = [jax.random.randint(jax.random.fold_in(rng, axis), (), 0, shape[axis]) for axis in range(len(shape))]
    result = result.at[tuple(place)].set(low)
    longest = shape.index(max(shape))
    place[longest] = (place[longest] + 1) % shape[longest]
    return result.at[tuple(place)].set(top_value)


def shard_levels(key, shape, shards, low, largest):
    def one(axis_at, shards_of):
        heights = jax.random.uniform(jax.random.fold_in(jax.random.fold_in(key, 6), axis_at), (shards_of,), jnp.float32, low / len(shards), largest / len(shards))
        return jnp.repeat(jnp.exp(heights), shape[axis_at] // shards_of).reshape((-1,) + (1,) * (len(shape) - axis_at - 1))

    factor_of = one(*shards[0])
    for cut in shards[1:]:
        factor_of = factor_of * one(*cut)
    return factor_of


def bell_draw(stream_key, extent, spread, bound, shards=(), kind=jnp.bfloat16):
    values = spread * jax.random.normal(stream_key, extent, jnp.float32)
    if shards:
        values = values * shard_levels(stream_key, extent, shards, -0.22, 0.18)
    return jnp.clip(values, -bound, bound).astype(kind)


def setup_inputs(seed: int = 0) -> dict:
    key_list = jax.random.split(jax.random.key(seed), 5)
    cycle_spectra = bell_draw(key_list[0], (2, M, NX, NY), 1.0, 6.0, ((1, 4), (2, 8)), jnp.float32)
    link_phase = place_ends(jax.random.randint(key_list[1], (2, NX, NY), 0, 64), jax.random.fold_in(key_list[1], 1), 0, 63).astype(jnp.int32)
    pump_mask = place_ends((jax.random.randint(key_list[2], (NX, NY), 0, 4) < 1).astype(jnp.int32), jax.random.fold_in(key_list[2], 1), 0, 1)
    detuning = jnp.clip(jax.random.uniform(key_list[3], (NX, NY), jnp.float32, -1.0, 1.0) * shard_levels(key_list[3], (NX, NY), ((0, 8),), -0.4, 0.0), -1.0, 1.0)
    return {"cycle_spectra": cycle_spectra, "link_phase": link_phase, "pump_mask": pump_mask, "detuning": detuning}


LOSS_RATE = 0.05
DISPERSION = 8.0
KERR_GAIN = 0.5
PUMP_LEVEL = 1.0
COUPLING = 0.35


def reorder(stored):
    row_count = stored.shape[1]
    col_count = stored.shape[2]
    shaped = stored.reshape(FACTOR, FACTOR, row_count, col_count)
    return shaped.transpose(1, 0, 2, 3).reshape(FACTOR * FACTOR, row_count, col_count)


def hop_field(values, along_first, along_second):
    upper_term = jnp.pad(values * along_first, ((0, 0), (1, 0), (0, 0)))[:, :-1]
    lower_term = jnp.pad(values, ((0, 0), (0, 1), (0, 0)))[:, 1:] * jnp.conj(along_first)
    before = jnp.pad(values * along_second, ((0, 0), (0, 0), (1, 0)))[:, :, :-1]
    after_term = jnp.pad(values, ((0, 0), (0, 0), (0, 1)))[:, :, 1:] * jnp.conj(along_second)
    return upper_term + lower_term + before + after_term


def couple(spectrum, along_first, along_second):
    def apply_block(mode_block):
        first_hop = hop_field(mode_block, along_first, along_second)
        second_hop = hop_field(first_hop, along_first, along_second)
        return mode_block - 1j * COUPLING * first_hop - (COUPLING * COUPLING / 2.0) * second_hop

    blocks = spectrum.reshape(FACTOR, FACTOR, spectrum.shape[1], spectrum.shape[2])
    return lax.map(apply_block, blocks).reshape(spectrum.shape)


def reference(cycle_spectra, link_phase, pump_mask, detuning):
    float_type = cycle_spectra.dtype
    angles = (2.0 * math.pi / 64.0) * link_phase.astype(float_type)
    along_first = jnp.cos(angles[0]) + 1j * jnp.sin(angles[0])
    along_second = jnp.cos(angles[1]) + 1j * jnp.sin(angles[1])
    spectrum = reorder(cycle_spectra[0]) + 1j * reorder(cycle_spectra[1])
    mode_number = jnp.arange(M, dtype=jnp.int32)
    scaled_mode = jnp.where(mode_number < M // 2, mode_number, mode_number - M).astype(float_type) / M
    pump_field = PUMP_LEVEL * pump_mask.astype(float_type)
    waveform = spectrum
    for round_index in range(ROUNDS):
        phase_turn = -(detuning[None] + DISPERSION * (scaled_mode * scaled_mode)[:, None, None])
        damping = math.exp(-LOSS_RATE)
        spectrum = spectrum * (damping * jnp.cos(phase_turn) + 1j * (damping * jnp.sin(phase_turn)))
        spectrum = couple(spectrum, along_first, along_second)
        waveform = jnp.fft.ifft(spectrum, axis=0, norm="ortho")
        intensity = waveform.real * waveform.real + waveform.imag * waveform.imag
        waveform = waveform * (jnp.cos(KERR_GAIN * intensity) + 1j * jnp.sin(KERR_GAIN * intensity)) + pump_field[None]
        if round_index + 1 < ROUNDS:
            spectrum = jnp.fft.fft(waveform, axis=0, norm="ortho")
    return jnp.stack([reorder(waveform.real), reorder(waveform.imag)])
```

```python
import functools
import math

import jax
import jax.numpy as jnp
import numpy as np
from jax import lax
from jax.experimental import pallas as pl
from jax.experimental.pallas import tpu as pltpu
from jax.sharding import Mesh, PartitionSpec as P

FACTOR = 64
M = FACTOR * FACTOR
LOSS_RATE = 0.05
DISPERSION = 8.0
KERR_GAIN = 0.5
PUMP_LEVEL = 1.0
COUPLING = 0.35

GROUP = ("yy", "mode")
LANES = 128
BF = jnp.bfloat16
F32 = jnp.float32
VMEM_LIMIT = 56 * 1024 * 1024


def split(x):
    hi = x.astype(BF)
    return hi, (x - hi.astype(F32)).astype(BF)


def dot3(a, b):
    ah, al = a if isinstance(a, tuple) else split(a)
    bh, bl = b if isinstance(b, tuple) else split(b)
    one = functools.partial(jnp.dot, preferred_element_type=F32)
    return one(ah, bh) + (one(ah, bl) + one(al, bh))


def kerr(re, im, pump):
    half = (0.5 * KERR_GAIN) * (re * re + im * im)
    n = jnp.floor(half * (1.0 / math.pi) + 0.5)
    r = half - n * 3.140625
    r = r - n * 0.0009670257568359375
    r = r - n * 6.2783295730096264e-07
    z = r * r
    s = r * (1.0 + z * (-1.0 / 6 + z * (1.0 / 120 + z * (-1.0 / 5040 + z * (1.0 / 362880 - z * (1.0 / 39916800))))))
    c = 1.0 + z * (-0.5 + z * (1.0 / 24 + z * (-1.0 / 720 + z * (1.0 / 40320 + z * (-1.0 / 3628800 + z * (1.0 / 479001600))))))
    sin = 2.0 * s * c
    cos = 1.0 - 2.0 * s * s
    return re * cos - im * sin + pump, re * sin + im * cos


def real_form(re, im):
    top = jnp.concatenate([re, -im], axis=-1)
    low = jnp.concatenate([im, re], axis=-1)
    return jnp.concatenate([top, low], axis=-2)


def mode_tables():
    idx = np.arange(FACTOR)
    w = np.exp(2j * np.pi * ((idx[:, None] * idx[None, :]) % FACTOR) / FACTOR)
    tw = np.exp(2j * np.pi * (idx[:, None] * idx[None, :]) / M)
    k = FACTOR * idx[None, :] + idx[:, None]
    mu = np.where(k < M // 2, k, k - M) / M
    disp = np.exp(-1j * DISPERSION * mu * mu)

    def pair(a):
        return jnp.asarray(a.real, F32), jnp.asarray(a.imag, F32)

    wr, wi = pair(w)
    left = pair(tw.T[:, :, None])
    right = pair(disp[:, None, :])
    fr = wr * right[0] - wi * right[1]
    fi = wr * right[1] + wi * right[0]
    mr = fr * left[0] - fi * left[1]
    mi = fr * left[1] + fi * left[0]
    first = real_form(mr, mi)
    second = real_form(*pair(w / FACTOR))
    back_left = pair(np.conj(tw)[:, :, None] / FACTOR)
    br = wr * back_left[0] + wi * back_left[1]
    bi = wr * back_left[1] - wi * back_left[0]
    back = real_form(br, bi)
    inverse = real_form(*pair(np.conj(w)))
    middle = jnp.einsum("oab,bc->oac", first, inverse, precision=lax.Precision.HIGHEST)
    return first, second, back, middle


def lattice_operator(sites, zz, block, rows_total, cols_total, rows, width):
    er, ec = rows + 4, width + 4
    padded = jnp.pad(sites, ((0, 0), (2, 2), (2, 2)))
    ext = lax.dynamic_slice(padded, (0, zz * rows, block * width), (sites.shape[0], er, ec))
    n = er * ec
    rr = (zz * rows - 2 + jnp.arange(er))[:, None]
    cc = (block * width - 2 + jnp.arange(ec))[None, :]
    live_r = (rr >= 0) & (rr < rows_total)
    live_c = (cc >= 0) & (cc < cols_total)
    a = 2.0 * math.pi / 64.0 * ext[:2]
    next_r = (rr + 1 >= 0) & (rr + 1 < rows_total)
    next_c = (cc + 1 >= 0) & (cc + 1 < cols_total)
    on0 = (live_r & next_r & live_c).astype(F32)
    on1 = (live_c & next_c & live_r).astype(F32)
    c0, s0 = ((on0 * jnp.cos(a[0])).reshape(n), (on0 * jnp.sin(a[0])).reshape(n))
    c1, s1 = ((on1 * jnp.cos(a[1])).reshape(n), (on1 * jnp.sin(a[1])).reshape(n))
    i = jnp.arange(n)[None, :]
    j = jnp.arange(n)[:, None]
    inner = (j % ec) != ec - 1
    inner_i = (i % ec) != ec - 1
    up = i == j + ec
    down = j == i + ec
    right = (i == j + 1) & inner
    left = (j == i + 1) & inner_i
    z = jnp.float32(0)
    hr = jnp.where(up, c0[:, None], z) + jnp.where(down, c0[None, :], z) + jnp.where(right, c1[:, None], z) + jnp.where(left, c1[None, :], z)
    hi = jnp.where(up, s0[:, None], z) - jnp.where(down, s0[None, :], z) + jnp.where(right, s1[:, None], z) - jnp.where(left, s1[None, :], z)

    def out_sites(h):
        return h.reshape(n, er, ec)[:, 2 : 2 + rows, 2 : 2 + width].reshape(n, rows * width)

    gr, gi = out_sites(hr), out_sites(hi)
    mm = functools.partial(jnp.matmul, precision=lax.Precision.HIGHEST)
    qr = mm(hr, gr) - mm(hi, gi)
    qi = mm(hr, gi) + mm(hi, gr)
    eye = out_sites((i == j).astype(F32))
    half = COUPLING * COUPLING / 2.0
    tr = eye + COUPLING * gi - half * qr
    ti = -COUPLING * gr - half * qi
    det = ext[2].reshape(n, 1)
    damp = math.exp(-LOSS_RATE)
    dr, di = damp * jnp.cos(det), -damp * jnp.sin(det)
    return (tr * dr - ti * di).reshape(er, ec, rows * width), (tr * di + ti * dr).reshape(er, ec, rows * width)


def operator_blocks(tr, ti, width):
    t = jnp.stack([jnp.stack([tr, ti], 2), jnp.stack([-ti, tr], 2)], 2)
    er = t.shape[0]
    kinds = er // 2
    main = t[:, 2 : 2 + width].reshape(kinds, 2, width, 2, 2, -1)
    main = main.transpose(0, 3, 1, 2, 4, 5).reshape(kinds, 2, 2 * width, 2, -1)
    edge = jnp.concatenate([t[:, :2], t[:, 2 + width :]], 1).reshape(kinds, 2, 4, 2, 2, -1)
    edge = edge.transpose(0, 3, 1, 2, 4, 5).reshape(kinds * 2 * 2 * 4, -1)
    return main, edge


def first_operator(main):
    zero = jnp.zeros_like(main)
    low = jnp.concatenate([main, zero], 2)
    high = jnp.concatenate([zero, main], 2)
    both = jnp.stack([low, high], 3)
    return both.reshape(both.shape[0] * 2 * LANES, -1)


def last_operator(main, edge):
    kinds = main.shape[0]
    half = LANES // 2
    m = main.reshape(kinds, 2, half, 2, 2, half)
    zero = jnp.zeros_like(m)
    h0 = jnp.concatenate([m, zero], -1)
    h1 = jnp.concatenate([zero, m], -1)
    own0 = jnp.concatenate([h0[1], h0[2]], 1).reshape(2 * LANES, -1)
    own1 = jnp.concatenate([h1[1], h1[2]], 1).reshape(2 * LANES, -1)
    up = jnp.concatenate([h0[0], h1[0]], 1).reshape(2 * LANES, -1)
    down = jnp.concatenate([h0[3], h1[3]], 1).reshape(2 * LANES, -1)
    e = edge.reshape(-1, 2, 2, half)
    ez = jnp.zeros_like(e)
    e0 = jnp.concatenate([e, ez], -1).reshape(edge.shape[0], -1)
    e1 = jnp.concatenate([ez, e], -1).reshape(edge.shape[0], -1)
    return jnp.concatenate([own0, own1, up, down], 0), jnp.stack([e0, e1])


def pack_kernel(x_ref, o_ref):
    h0, h1 = x_ref[0, 0], x_ref[0, 1]
    cols = h0.shape[1] // 2
    w = LANES // 4
    for d in range(cols // w):
        lo = slice(w * d, w * d + w)
        hi = slice(cols + w * d, cols + w * d + w)
        o_ref[d, 0] = jnp.concatenate([h0[:, lo], h0[:, hi], h1[:, lo], h1[:, hi]], axis=1)


def unpack_kernel(x_ref, o_ref):
    w = LANES // 4
    count = x_ref.shape[0]
    for h in range(2):
        parts = []
        for r in range(2):
            for d in range(count):
                at = (2 * h + r) * w
                parts.append(x_ref[d, 0, :, at : at + w])
        o_ref[0, h] = jnp.concatenate(parts, axis=1)


def first_kernel(own_ref, up_ref, down_ref, edge_ref, t_ref, te_ref, m_ref, o_ref):
    parts = [up_ref[0, 0], up_ref[0, 1], own_ref[0, 0, 0], own_ref[0, 0, 1]]
    parts += [own_ref[1, 0, 0], own_ref[1, 0, 1], down_ref[0, 0], down_ref[0, 1]]
    x = jnp.concatenate(parts, axis=1)
    n = x.shape[0]
    y = dot3(x, t_ref[...])
    e = edge_ref[0].T
    te = split(te_ref[...])
    for h in range(2):
        yh = y[:, 2 * LANES * h : 2 * LANES * (h + 1)] + dot3(e[n * h : n * (h + 1)], te)
        for o in range(n // FACTOR):
            rows = slice(FACTOR * o, FACTOR * (o + 1))
            b = jnp.concatenate([yh[rows, :LANES], yh[rows, LANES:]], axis=0)
            at = h * (n // FACTOR) + o
            o_ref[at] = dot3(m_ref[at], b).reshape(2, FACTOR, LANES)


def gather_rows(ref, at):
    return jnp.concatenate([ref[:, 0, at, :], ref[:, 1, at, :]], axis=0)


def middle_kernel(a_ref, f_ref, back_ref, mid_ref, pump_ref, w_ref, mid_scratch):
    f = split(f_ref[...])
    pump = pump_ref[...]

    def one(s, _):
        w = dot3(f, gather_rows(a_ref, s))
        re, im = kerr(w[:FACTOR], w[FACTOR:], pump)
        v = dot3(back_ref[s], jnp.concatenate([re, im], axis=0))
        w_ref[s] = v.reshape(2, FACTOR, LANES)
        return 0

    lax.fori_loop(0, FACTOR, one, 0, unroll=2)

    def two(o, _):
        v = dot3(mid_ref[o], gather_rows(w_ref, o))
        mid_scratch[o] = v.reshape(2, FACTOR, LANES)
        return 0

    lax.fori_loop(0, FACTOR, two, 0, unroll=2)

    def three(s, _):
        w_ref[s] = dot3(f, gather_rows(mid_scratch, s)).reshape(2, FACTOR, LANES)
        return 0

    lax.fori_loop(0, FACTOR, three, 0, unroll=2)


def last_kernel(w_ref, up_ref, down_ref, edge_ref, t_ref, te_ref, pump_ref, o_ref):
    n8 = up_ref.shape[0]
    n = n8 * FACTOR

    def flat(ref, lo, c):
        return ref[lo : lo + n8, c].reshape(n, LANES)

    parts = [flat(w_ref, n8 * h, c) for h in range(2) for c in range(2)]
    parts += [flat(up_ref, 0, c) for c in range(2)] + [flat(down_ref, 0, c) for c in range(2)]
    y = dot3(jnp.concatenate(parts, axis=1), t_ref[...])
    e = edge_ref[...].T
    for h in range(2):
        y = y + dot3(e[n * h : n * (h + 1)], te_ref[h])
    for half in range(2):
        re = y[:, LANES * half : LANES * (half + 1)]
        im = y[:, LANES * (2 + half) : LANES * (3 + half)]
        re, im = kerr(re, im, pump_ref[half : half + 1])
        o_ref[half, 0, 0] = re
        o_ref[half, 0, 1] = im


def params():
    return pltpu.CompilerParams(vmem_limit_bytes=VMEM_LIMIT)


def whole(shape):
    return pl.BlockSpec(shape, lambda *_: (0,) * len(shape))


def body(tiles, groups, cycle_spectra, link_phase, pump_mask, detuning):
    modes, rows_in, cols = cycle_spectra.shape[1:]
    devices = 2 * groups
    width = cols // devices
    rows = 2 * rows_in
    half = modes // 2
    outer = modes // FACTOR
    zz = lax.axis_index("zz")
    block = lax.axis_index("yy") * groups + lax.axis_index("mode")
    up_perm = [(i, i + 1) for i in range(tiles - 1)]
    down_perm = [(i + 1, i) for i in range(tiles - 1)]

    def to_group(x):
        return lax.all_to_all(x, GROUP, split_axis=0, concat_axis=0, tiled=True)

    sites = jnp.concatenate([link_phase.astype(F32), detuning[None], pump_mask.astype(F32)[None]], 0)
    sites = lax.all_gather(sites, ("zz", "yy"), axis=1, tiled=True)
    tr, ti = lattice_operator(sites, zz, block, tiles * rows, cols, rows, width)
    main, edge_op = operator_blocks(tr, ti, width)
    t_first = first_operator(main)
    t_last, edge_last = last_operator(main, edge_op)
    pump = PUMP_LEVEL * lax.dynamic_slice(sites[3], (zz * rows, block * width), (rows, width))
    pump_flat = pump.reshape(1, rows * width)
    pump_half = pump.reshape(2, LANES // 2)
    pump_last = jnp.concatenate([pump_half, pump_half], 1)
    m_first, second, back, middle = mode_tables()

    flat = cycle_spectra.reshape(2, 2, half, rows_in * cols)
    steps = 4
    packed = pl.pallas_call(
        pack_kernel,
        grid=(2, steps),
        in_specs=[pl.BlockSpec((1, 2, half // steps, rows_in * cols), lambda c, i: (c, 0, i, 0))],
        out_specs=pl.BlockSpec((devices, 1, half // steps, LANES), lambda c, i: (0, c, i, 0)),
        out_shape=jax.ShapeDtypeStruct((devices, 2, half, LANES), F32),
        compiler_params=params(),
    )(flat)
    own = to_group(packed)
    own = own.reshape(2, groups, 2, half, LANES)
    cells = cycle_spectra.reshape(2, modes, rows_in, devices, width)
    none = jnp.zeros((2, modes, rows_in, 1, 2), F32)
    from_left = jnp.concatenate([none, cells[:, :, :, :-1, width - 2 :]], 3)
    from_right = jnp.concatenate([cells[:, :, :, 1:, :2], none], 3)
    rim = jnp.concatenate([from_left, from_right], 4).transpose(3, 0, 2, 4, 1)
    rim = to_group(rim.reshape(devices, 2 * rows_in * 4, modes)).reshape(2, groups, 2 * rows_in * 4, modes)
    up = lax.ppermute(own[1], "zz", up_perm)
    down = lax.ppermute(own[0], "zz", down_perm)
    rim_up = lax.ppermute(rim[1], "zz", up_perm)
    rim_down = lax.ppermute(rim[0], "zz", down_perm)
    edge = jnp.concatenate([rim_up, rim[0], rim[1], rim_down], 1)

    stage = pl.pallas_call(
        first_kernel,
        grid=(groups,),
        in_specs=[
            pl.BlockSpec((2, 1, 2, half, LANES), lambda g: (0, g, 0, 0, 0)),
            pl.BlockSpec((1, 2, half, LANES), lambda g: (g, 0, 0, 0)),
            pl.BlockSpec((1, 2, half, LANES), lambda g: (g, 0, 0, 0)),
            pl.BlockSpec((1,) + edge.shape[1:], lambda g: (g, 0, 0)),
            whole(t_first.shape),
            whole(edge_op.shape),
            pl.BlockSpec((outer, LANES, LANES), lambda g: (g, 0, 0)),
        ],
        out_specs=pl.BlockSpec((outer, 2, FACTOR, LANES), lambda g: (g, 0, 0, 0)),
        out_shape=jax.ShapeDtypeStruct((FACTOR, 2, FACTOR, LANES), F32),
        compiler_params=params(),
    )(own, up, down, edge, t_first, edge_op, m_first)

    wave = pl.pallas_call(
        middle_kernel,
        out_shape=jax.ShapeDtypeStruct((FACTOR, 2, FACTOR, LANES), F32),
        scratch_shapes=[pltpu.VMEM((FACTOR, 2, FACTOR, LANES), F32)],
        compiler_params=params(),
    )(stage, second, back, middle, pump_flat)

    cut = LANES // 2
    parts = wave.reshape(groups, 2, outer // 2, 2, FACTOR, LANES)
    up = jnp.concatenate([parts[:, 0, ..., cut:], parts[:, 1, ..., cut:]], -1)
    down = jnp.concatenate([parts[:, 0, ..., :cut], parts[:, 1, ..., :cut]], -1)
    half_shape = (FACTOR // 2, 2, FACTOR, LANES)
    up = lax.ppermute(up.reshape(half_shape), "zz", up_perm)
    down = lax.ppermute(down.reshape(half_shape), "zz", down_perm)
    right_perm = [(i, i + 1) for i in range(devices - 1)]
    left_perm = [(i + 1, i) for i in range(devices - 1)]
    rims = wave.reshape(FACTOR, 2, FACTOR, rows, width)
    to_right = rims[..., width - 2 :].transpose(1, 3, 4, 0, 2).reshape(2, rows, 2, M)
    to_left = rims[..., :2].transpose(1, 3, 4, 0, 2).reshape(2, rows, 2, M)
    rim = jnp.concatenate([lax.ppermute(to_right, GROUP, right_perm), lax.ppermute(to_left, GROUP, left_perm)], 2)
    rim = rim.reshape(2, 2, 2, 4, M).transpose(1, 0, 2, 3, 4)
    rim_up = lax.ppermute(rim[1], "zz", up_perm)
    rim_down = lax.ppermute(rim[0], "zz", down_perm)
    edge = jnp.concatenate([rim_up, rim[0], rim[1], rim_down], 0).reshape(-1, M)

    out = pl.pallas_call(
        last_kernel,
        grid=(groups,),
        in_specs=[
            pl.BlockSpec((outer, 2, FACTOR, LANES), lambda g: (g, 0, 0, 0)),
            pl.BlockSpec((outer // 2, 2, FACTOR, LANES), lambda g: (g, 0, 0, 0)),
            pl.BlockSpec((outer // 2, 2, FACTOR, LANES), lambda g: (g, 0, 0, 0)),
            pl.BlockSpec((edge.shape[0], modes), lambda g: (0, g)),
            whole(t_last.shape),
            whole(edge_last.shape),
            whole(pump_last.shape),
        ],
        out_specs=pl.BlockSpec((2, 1, 2, half, LANES), lambda g: (0, g, 0, 0, 0)),
        out_shape=jax.ShapeDtypeStruct((2, groups, 2, half, LANES), F32),
        compiler_params=params(),
    )(wave, up, down, edge, t_last, edge_last, pump_last)
    got = to_group(out.reshape(devices, 2, half, LANES))
    samples = pl.pallas_call(
        unpack_kernel,
        grid=(2, steps),
        in_specs=[pl.BlockSpec((devices, 1, half // steps, LANES), lambda c, i: (0, c, i, 0))],
        out_specs=pl.BlockSpec((1, 2, half // steps, rows_in * cols), lambda c, i: (c, 0, i, 0)),
        out_shape=jax.ShapeDtypeStruct((2, 2, half, rows_in * cols), F32),
        compiler_params=params(),
    )(got)
    return samples.reshape(2, modes, rows_in, cols)


def solution(mesh):
    names = mesh.axis_names
    tiles, groups = mesh.shape[names[0]], mesh.shape[names[1]]
    paired = Mesh(mesh.devices.reshape(tiles // 2, 2, groups), ("zz", "yy", "mode"))
    tile = ("zz", "yy")
    return jax.shard_map(
        functools.partial(body, tiles // 2, groups),
        mesh=paired,
        in_specs=(
            P(None, "mode", tile, None),
            P(None, tile, None),
            P(tile, None),
            P(tile, None),
        ),
        out_specs=P(None, "mode", tile, None),
        check_vma=False,
    )
```

```python
import functools
import math

import jax
import jax.numpy as jnp
import numpy as np
from jax import lax
from jax.experimental import pallas as pl
from jax.experimental.pallas import tpu as pltpu
from jax.sharding import Mesh, PartitionSpec as P

FACTOR = 64
M = FACTOR * FACTOR
LOSS_RATE = 0.05
DISPERSION = 8.0
KERR_GAIN = 0.5
PUMP_LEVEL = 1.0
COUPLING = 0.35
CHUNKS = 4

GROUP = ("yy", "mode")
LANES = 128
BF = jnp.bfloat16
F32 = jnp.float32
VMEM_LIMIT = 56 * 1024 * 1024


def split(x):
    hi = x.astype(BF)
    return hi, (x - hi.astype(F32)).astype(BF)


def dot3(a, b):
    ah, al = a if isinstance(a, tuple) else split(a)
    bh, bl = b if isinstance(b, tuple) else split(b)
    one = functools.partial(jnp.dot, preferred_element_type=F32)
    return one(ah, bh) + (one(ah, bl) + one(al, bh))


def kerr(re, im, pump):
    half = (0.5 * KERR_GAIN) * (re * re + im * im)
    n = jnp.floor(half * (1.0 / math.pi) + 0.5)
    r = half - n * 3.140625
    r = r - n * 0.0009670257568359375
    r = r - n * 6.2783295730096264e-07
    z = r * r
    s = r * (1.0 + z * (-1.0 / 6 + z * (1.0 / 120 + z * (-1.0 / 5040 + z * (1.0 / 362880 - z * (1.0 / 39916800))))))
    c = 1.0 + z * (-0.5 + z * (1.0 / 24 + z * (-1.0 / 720 + z * (1.0 / 40320 + z * (-1.0 / 3628800 + z * (1.0 / 479001600))))))
    sin = 2.0 * s * c
    cos = 1.0 - 2.0 * s * s
    return re * cos - im * sin + pump, re * sin + im * cos


def real_form(re, im):
    top = jnp.concatenate([re, -im], axis=-1)
    low = jnp.concatenate([im, re], axis=-1)
    return jnp.concatenate([top, low], axis=-2)


def mode_tables():
    idx = np.arange(FACTOR)
    w = np.exp(2j * np.pi * ((idx[:, None] * idx[None, :]) % FACTOR) / FACTOR)
    tw = np.exp(2j * np.pi * (idx[:, None] * idx[None, :]) / M)
    k = FACTOR * idx[None, :] + idx[:, None]
    mu = np.where(k < M // 2, k, k - M) / M
    disp = np.exp(-1j * DISPERSION * mu * mu)

    def pair(a):
        return jnp.asarray(a.real, F32), jnp.asarray(a.imag, F32)

    wr, wi = pair(w)
    left = pair(tw.T[:, :, None])
    right = pair(disp[:, None, :])
    fr = wr * right[0] - wi * right[1]
    fi = wr * right[1] + wi * right[0]
    mr = fr * left[0] - fi * left[1]
    mi = fr * left[1] + fi * left[0]
    first = real_form(mr, mi)
    second = real_form(*pair(w / FACTOR))
    back_left = pair(np.conj(tw)[:, :, None] / FACTOR)
    br = wr * back_left[0] + wi * back_left[1]
    bi = wr * back_left[1] - wi * back_left[0]
    back = real_form(br, bi)
    inverse = real_form(*pair(np.conj(w)))
    middle = jnp.einsum("oab,bc->oac", first, inverse, precision=lax.Precision.HIGHEST)
    return first, second, back, middle


def lattice_operator(sites, zz, block, rows_total, cols_total, rows, width):
    er, ec = rows + 4, width + 4
    padded = jnp.pad(sites, ((0, 0), (2, 2), (2, 2)))
    ext = lax.dynamic_slice(padded, (0, zz * rows, block * width), (sites.shape[0], er, ec))
    n = er * ec
    rr = (zz * rows - 2 + jnp.arange(er))[:, None]
    cc = (block * width - 2 + jnp.arange(ec))[None, :]
    live_r = (rr >= 0) & (rr < rows_total)
    live_c = (cc >= 0) & (cc < cols_total)
    a = 2.0 * math.pi / 64.0 * ext[:2]
    next_r = (rr + 1 >= 0) & (rr + 1 < rows_total)
    next_c = (cc + 1 >= 0) & (cc + 1 < cols_total)
    on0 = (live_r & next_r & live_c).astype(F32)
    on1 = (live_c & next_c & live_r).astype(F32)
    c0, s0 = ((on0 * jnp.cos(a[0])).reshape(n), (on0 * jnp.sin(a[0])).reshape(n))
    c1, s1 = ((on1 * jnp.cos(a[1])).reshape(n), (on1 * jnp.sin(a[1])).reshape(n))
    i = jnp.arange(n)[None, :]
    j = jnp.arange(n)[:, None]
    inner = (j % ec) != ec - 1
    inner_i = (i % ec) != ec - 1
    up = i == j + ec
    down = j == i + ec
    right = (i == j + 1) & inner
    left = (j == i + 1) & inner_i
    z = jnp.float32(0)
    hr = jnp.where(up, c0[:, None], z) + jnp.where(down, c0[None, :], z) + jnp.where(right, c1[:, None], z) + jnp.where(left, c1[None, :], z)
    hi = jnp.where(up, s0[:, None], z) - jnp.where(down, s0[None, :], z) + jnp.where(right, s1[:, None], z) - jnp.where(left, s1[None, :], z)

    def out_sites(h):
        return h.reshape(n, er, ec)[:, 2 : 2 + rows, 2 : 2 + width].reshape(n, rows * width)

    gr, gi = out_sites(hr), out_sites(hi)
    mm = functools.partial(jnp.matmul, precision=lax.Precision.HIGHEST)
    qr = mm(hr, gr) - mm(hi, gi)
    qi = mm(hr, gi) + mm(hi, gr)
    eye = out_sites((i == j).astype(F32))
    half = COUPLING * COUPLING / 2.0
    tr = eye + COUPLING * gi - half * qr
    ti = -COUPLING * gr - half * qi
    det = ext[2].reshape(n, 1)
    damp = math.exp(-LOSS_RATE)
    dr, di = damp * jnp.cos(det), -damp * jnp.sin(det)
    return (tr * dr - ti * di).reshape(er, ec, rows * width), (tr * di + ti * dr).reshape(er, ec, rows * width)


def operator_blocks(tr, ti, width):
    t = jnp.stack([jnp.stack([tr, ti], 2), jnp.stack([-ti, tr], 2)], 2)
    er = t.shape[0]
    kinds = er // 2
    main = t[:, 2 : 2 + width].reshape(kinds, 2, width, 2, 2, -1)
    main = main.transpose(0, 3, 1, 2, 4, 5).reshape(kinds, 2, 2 * width, 2, -1)
    edge = jnp.concatenate([t[:, :2], t[:, 2 + width :]], 1).reshape(kinds, 2, 4, 2, 2, -1)
    edge = edge.transpose(0, 3, 1, 2, 4, 5).reshape(kinds * 2 * 2 * 4, -1)
    return main, edge


def first_operator(main):
    zero = jnp.zeros_like(main)
    low = jnp.concatenate([main, zero], 2)
    high = jnp.concatenate([zero, main], 2)
    both = jnp.stack([low, high], 3)
    return both.reshape(both.shape[0] * 2 * LANES, -1)


def last_operator(main, edge):
    kinds = main.shape[0]
    half = LANES // 2
    m = main.reshape(kinds, 2, half, 2, 2, half)
    zero = jnp.zeros_like(m)
    h0 = jnp.concatenate([m, zero], -1)
    h1 = jnp.concatenate([zero, m], -1)
    own0 = jnp.concatenate([h0[1], h0[2]], 1).reshape(2 * LANES, -1)
    own1 = jnp.concatenate([h1[1], h1[2]], 1).reshape(2 * LANES, -1)
    up = jnp.concatenate([h0[0], h1[0]], 1).reshape(2 * LANES, -1)
    down = jnp.concatenate([h0[3], h1[3]], 1).reshape(2 * LANES, -1)
    e = edge.reshape(-1, 2, 2, half)
    ez = jnp.zeros_like(e)
    e0 = jnp.concatenate([e, ez], -1).reshape(edge.shape[0], -1)
    e1 = jnp.concatenate([ez, e], -1).reshape(edge.shape[0], -1)
    return jnp.concatenate([own0, own1, up, down], 0), jnp.stack([e0, e1])


def pack_kernel(x_ref, *o_refs):
    rows = [x_ref[0, h, :, r, :] for h in range(2) for r in range(2)]
    cols = rows[0].shape[1]
    w = LANES // 4
    for d in range(cols // w):
        got = jnp.concatenate([x[:, w * d : w * d + w] for x in rows], axis=1)
        n = got.shape[0] // len(o_refs)
        for i, o_ref in enumerate(o_refs):
            o_ref[d, 0] = got[n * i : n * (i + 1)]


def unpack_kernel(*refs):
    o_ref = refs[-1]
    w = LANES // 4
    count, _, n, _ = refs[0].shape
    for i, x_ref in enumerate(refs[:-1]):
        for h in range(2):
            for r in range(2):
                at = (2 * h + r) * w
                parts = [x_ref[d, 0, :, at : at + w] for d in range(count)]
                o_ref[0, h, n * i : n * (i + 1), r, :] = jnp.concatenate(parts, axis=1)


def wide(a):
    hi, lo = split(a)
    return jnp.concatenate([hi, lo, hi], axis=-1)


def dot_wide(a, b):
    hi, lo = split(b)
    return jnp.dot(a, jnp.concatenate([hi, hi, lo], axis=0), preferred_element_type=F32)


def first_kernel(index, own_ref, up_ref, down_ref, edge_ref, t_ref, te_ref, m_ref, o_ref):
    groups, _, n, _ = up_ref.shape
    half = edge_ref.shape[2] // 2

    def flat(x):
        return x.reshape(groups * n, LANES)

    parts = [up_ref[:, c] for c in range(2)] + [own_ref[y, :, c] for y in range(2) for c in range(2)]
    parts += [down_ref[:, c] for c in range(2)]
    y = dot3(jnp.concatenate([flat(x) for x in parts], axis=1), t_ref[...])
    te = split(te_ref[...])
    for h in range(2):
        at = half * h + n * index
        e = jnp.concatenate([edge_ref[g, :, at : at + n] for g in range(groups)], axis=1).T
        yh = y[:, 2 * LANES * h : 2 * LANES * (h + 1)] + dot3(e, te)
        for g in range(groups):
            for o in range(n // FACTOR):
                low = g * n + FACTOR * o
                rows = slice(low, low + FACTOR)
                b = jnp.concatenate([yh[rows, :LANES], yh[rows, LANES:]], axis=0)
                o_ref[g, h, o] = dot_wide(wide(m_ref[g, h, 0, o]), b).reshape(2, FACTOR, LANES)


def gather_rows(refs, at):
    return jnp.concatenate([r[:, c, at, :] for c in range(2) for r in refs], axis=0)


def middle_kernel(chunks, f1_ref, f_ref, back_ref, mid_ref, pump_ref, *refs):
    a_refs = refs[:chunks]
    w_ref = refs[chunks]
    ups = refs[chunks + 1 : 2 * chunks + 1]
    downs = refs[2 * chunks + 1 : 3 * chunks + 1]
    v_scratch, mid_scratch = refs[3 * chunks + 1 :]
    f1 = wide(f1_ref[...])
    f = wide(f_ref[...])
    pump = pump_ref[...]
    batch = 4

    def one(i, _):
        w = dot_wide(f1, jnp.concatenate([gather_rows(a_refs, i * batch + j) for j in range(batch)], axis=1))
        for j in range(batch):
            wj = w[:, LANES * j : LANES * (j + 1)]
            re, im = kerr(wj[:FACTOR], wj[FACTOR:], pump)
            v = dot_wide(wide(back_ref[i * batch + j]), jnp.concatenate([re, im], axis=0))
            v_scratch[i * batch + j] = v.reshape(2, FACTOR, LANES)
        return 0

    lax.fori_loop(0, FACTOR // batch, one, 0)

    def two(i, _):
        for j in range(batch):
            o = i * batch + j
            v = dot_wide(wide(mid_ref[o]), gather_rows([v_scratch], o))
            mid_scratch[o] = v.reshape(2, FACTOR, LANES)
        return 0

    lax.fori_loop(0, FACTOR // batch, two, 0)

    groups = w_ref.shape[0]
    size = ups[0].shape[0] // groups
    cut = LANES // 2
    for c in range(chunks):

        def three(g, _):
            s = [g * (2 * size * chunks) + h * (size * chunks) + c * size + j for h in range(2) for j in range(size)]
            w = dot_wide(f, jnp.concatenate([gather_rows([mid_scratch], at) for at in s], axis=1))
            for j in range(size):
                w0 = w[:, LANES * j : LANES * (j + 1)]
                w1 = w[:, LANES * (size + j) : LANES * (size + j + 1)]
                w_ref[g, 0, c, j] = w0.reshape(2, FACTOR, LANES)
                w_ref[g, 1, c, j] = w1.reshape(2, FACTOR, LANES)
                up = jnp.concatenate([w0[:, cut:], w1[:, cut:]], axis=1)
                down = jnp.concatenate([w0[:, :cut], w1[:, :cut]], axis=1)
                ups[c][g * size + j] = up.reshape(2, FACTOR, LANES)
                downs[c][g * size + j] = down.reshape(2, FACTOR, LANES)
            return 0

        lax.fori_loop(0, groups, three, 0)


def last_kernel(index, w_ref, up_ref, down_ref, edge_ref, t_ref, te_ref, pump_ref, o_ref):
    groups = w_ref.shape[0]
    n = w_ref.shape[3] * FACTOR
    total = groups * n
    half = edge_ref.shape[1] // groups // 2

    parts = [w_ref[:, h, 0, :, c].reshape(total, LANES) for h in range(2) for c in range(2)]
    parts += [ref[:, c].reshape(total, LANES) for ref in (up_ref, down_ref) for c in range(2)]
    y = dot3(jnp.concatenate(parts, axis=1), t_ref[...])
    for h in range(2):
        lows = [(2 * g + h) * half + n * index for g in range(groups)]
        e = jnp.concatenate([edge_ref[:, at : at + n] for at in lows], axis=1).T
        y = y + dot3(e, te_ref[h])
    for side in range(2):
        re = y[:, LANES * side : LANES * (side + 1)]
        im = y[:, LANES * (2 + side) : LANES * (3 + side)]
        re, im = kerr(re, im, pump_ref[side : side + 1])
        o_ref[side, :, 0] = re.reshape(groups, n, LANES)
        o_ref[side, :, 1] = im.reshape(groups, n, LANES)


def params():
    return pltpu.CompilerParams(vmem_limit_bytes=VMEM_LIMIT)


def whole(shape):
    return pl.BlockSpec(shape, lambda *_: (0,) * len(shape))


def body(tiles, groups, cycle_spectra, link_phase, pump_mask, detuning):
    modes, rows_in, cols = cycle_spectra.shape[1:]
    devices = 2 * groups
    width = cols // devices
    rows = 2 * rows_in
    half = modes // 2
    outer = modes // FACTOR
    zz = lax.axis_index("zz")
    block = lax.axis_index("yy") * groups + lax.axis_index("mode")
    up_perm = [(i, i + 1) for i in range(tiles - 1)]
    down_perm = [(i + 1, i) for i in range(tiles - 1)]

    def to_group(x):
        return lax.all_to_all(x, GROUP, split_axis=0, concat_axis=0, tiled=True)

    sites = jnp.concatenate([link_phase.astype(F32), detuning[None], pump_mask.astype(F32)[None]], 0)
    sites = lax.all_gather(sites, ("zz", "yy"), axis=1, tiled=True)
    sites, cycle_spectra = lax.optimization_barrier((sites, cycle_spectra))
    tr, ti = lattice_operator(sites, zz, block, tiles * rows, cols, rows, width)
    main, edge_op = operator_blocks(tr, ti, width)
    t_first = first_operator(main)
    t_last, edge_last = last_operator(main, edge_op)
    pump = PUMP_LEVEL * lax.dynamic_slice(sites[3], (zz * rows, block * width), (rows, width))
    pump_flat = pump.reshape(1, rows * width)
    pump_half = pump.reshape(2, LANES // 2)
    pump_last = jnp.concatenate([pump_half, pump_half], 1)
    m_first, second, back, middle = mode_tables()

    everyone = ("zz",) + GROUP
    cells = cycle_spectra.reshape(2, modes, rows_in, devices, width)
    none = jnp.zeros((2, modes, rows_in, 1, 2), F32)
    from_left = jnp.concatenate([none, cells[:, :, :, :-1, width - 2 :]], 3)
    from_right = jnp.concatenate([cells[:, :, :, 1:, :2], none], 3)
    rim = jnp.concatenate([from_left, from_right], 4).transpose(3, 0, 2, 4, 1)
    chunks = CHUNKS
    part = half // chunks
    packed = pl.pallas_call(
        pack_kernel,
        grid=(2,),
        in_specs=[pl.BlockSpec((1, 2, half, rows_in, cols), lambda c: (c, 0, 0, 0, 0))],
        out_specs=[pl.BlockSpec((devices, 1, part, LANES), lambda c: (0, c, 0, 0))] * chunks,
        out_shape=[jax.ShapeDtypeStruct((devices, 2, part, LANES), F32)] * chunks,
        compiler_params=params(),
    )(cycle_spectra.reshape(2, 2, half, rows_in, cols))
    rim = to_group(rim.reshape(devices, 2 * rows_in * 4, modes)).reshape(2, groups, 2 * rows_in * 4, modes)
    rim_up = lax.ppermute(rim[1], "zz", up_perm)
    rim_down = lax.ppermute(rim[0], "zz", down_perm)
    edge = jnp.concatenate([rim_up, rim[0], rim[1], rim_down], 1)
    small = part // FACTOR
    m_view = m_first.reshape(groups, 2, chunks, small, LANES, LANES)
    stages = []
    for i in range(chunks):
        own = to_group(packed[i]).reshape(2, groups, 2, part, LANES)
        up = lax.ppermute(own[1], "zz", up_perm)
        down = lax.ppermute(own[0], "zz", down_perm)
        stage = pl.pallas_call(
            functools.partial(first_kernel, i),
            grid=(1,),
            in_specs=[
                whole(own.shape),
                whole(up.shape),
                whole(down.shape),
                whole(edge.shape),
                whole(t_first.shape),
                whole(edge_op.shape),
                pl.BlockSpec((groups, 2, 1, small, LANES, LANES), lambda _, i=i: (0, 0, i, 0, 0, 0)),
            ],
            out_specs=whole((groups, 2, small, 2, FACTOR, LANES)),
            out_shape=jax.ShapeDtypeStruct((groups, 2, small, 2, FACTOR, LANES), F32),
            compiler_params=params(),
        )(own, up, down, edge, t_first, edge_op, m_view)
        stages.append(stage.reshape(FACTOR // chunks, 2, FACTOR, LANES))
    second_first = second.reshape(2 * FACTOR, 2, groups, 2, chunks, small)
    second_first = second_first.transpose(0, 1, 4, 2, 3, 5).reshape(second.shape)

    each = outer // 2 // chunks
    halo_shape = jax.ShapeDtypeStruct((groups * each, 2, FACTOR, LANES), F32)
    full = (FACTOR, 2, FACTOR, LANES)
    wave_shape = (groups, 2, chunks, each, 2, FACTOR, LANES)
    got = pl.pallas_call(
        functools.partial(middle_kernel, chunks),
        out_shape=[jax.ShapeDtypeStruct(wave_shape, F32)] + [halo_shape] * (2 * chunks),
        scratch_shapes=[pltpu.VMEM(full, F32), pltpu.VMEM(full, F32)],
        compiler_params=params(),
    )(second_first, second, back, middle, pump_flat, *stages)
    wave, ups, downs = got[0], got[1 : chunks + 1], got[chunks + 1 :]

    rims = wave.reshape(FACTOR, 2, FACTOR, rows, width)
    sides = []
    for low, step in ((width - 2, 1), (0, -1)):
        cells = rims[..., low : low + 2].transpose(3, 1, 4, 0, 2).reshape(2, 2, 2, 2, M)
        took = []
        for source, turn in ((1, 1), (None, 0), (0, -1)):
            perm = []
            for at in range(tiles):
                for d in range(devices):
                    if 0 <= at + turn < tiles and 0 <= d + step < devices:
                        perm.append((at * devices + d, (at + turn) * devices + d + step))
            sent = cells if source is None else cells[source : source + 1]
            took.append(lax.ppermute(sent, everyone, perm))
        sides.append(jnp.concatenate(took, 0))
    edge = jnp.concatenate(sides, 3).transpose(0, 2, 1, 3, 4).reshape(-1, M)

    arrived = []
    for i in range(chunks):
        up = lax.ppermute(ups[i], "zz", up_perm)
        down = lax.ppermute(downs[i], "zz", down_perm)
        out = pl.pallas_call(
            functools.partial(last_kernel, i),
            grid=(1,),
            in_specs=[
                pl.BlockSpec((groups, 2, 1, each, 2, FACTOR, LANES), lambda _, i=i: (0, 0, i, 0, 0, 0, 0)),
                whole(up.shape),
                whole(down.shape),
                whole(edge.shape),
                whole(t_last.shape),
                whole(edge_last.shape),
                whole(pump_last.shape),
            ],
            out_specs=whole((2, groups, 2, part, LANES)),
            out_shape=jax.ShapeDtypeStruct((2, groups, 2, part, LANES), F32),
            compiler_params=params(),
        )(wave, up, down, edge, t_last, edge_last, pump_last)
        arrived.append(to_group(out.reshape(devices, 2, part, LANES)))
    samples = pl.pallas_call(
        unpack_kernel,
        grid=(2,),
        in_specs=[pl.BlockSpec((devices, 1, part, LANES), lambda c: (0, c, 0, 0))] * chunks,
        out_specs=pl.BlockSpec((1, 2, half, rows_in, cols), lambda c: (c, 0, 0, 0, 0)),
        out_shape=jax.ShapeDtypeStruct((2, 2, half, rows_in, cols), F32),
        compiler_params=params(),
    )(*arrived)
    return samples.reshape(2, modes, rows_in, cols)


def solution(mesh):
    names = mesh.axis_names
    tiles, groups = mesh.shape[names[0]], mesh.shape[names[1]]
    paired = Mesh(mesh.devices.reshape(tiles // 2, 2, groups), ("zz", "yy", "mode"))
    tile = ("zz", "yy")
    return jax.shard_map(
        functools.partial(body, tiles // 2, groups),
        mesh=paired,
        in_specs=(
            P(None, "mode", tile, None),
            P(None, tile, None),
            P(tile, None),
            P(tile, None),
        ),
        out_specs=P(None, "mode", tile, None),
        check_vma=False,
    )
```

```python
import functools
import math

import jax
import jax.numpy as jnp
import numpy as np
from jax import lax
from jax.experimental import pallas as pl
from jax.experimental.pallas import tpu as pltpu
from jax.sharding import Mesh, PartitionSpec as P

FACTOR = 64
M = FACTOR * FACTOR
LOSS_RATE = 0.05
DISPERSION = 8.0
KERR_GAIN = 0.5
PUMP_LEVEL = 1.0
COUPLING = 0.35

MESH = pl.DeviceIdType.MESH
GROUP = ("yy", "mode")
LANES = 128
BF = jnp.bfloat16
F32 = jnp.float32
VMEM_LIMIT = 56 * 1024 * 1024


def split(x):
    hi = x.astype(BF)
    return hi, (x - hi.astype(F32)).astype(BF)


def dot3(a, b):
    ah, al = a if isinstance(a, tuple) else split(a)
    bh, bl = b if isinstance(b, tuple) else split(b)
    one = functools.partial(jnp.dot, preferred_element_type=F32)
    return one(ah, bh) + (one(ah, bl) + one(al, bh))


def kerr(re, im, pump):
    half = (0.5 * KERR_GAIN) * (re * re + im * im)
    n = jnp.floor(half * (1.0 / math.pi) + 0.5)
    r = half - n * 3.140625
    r = r - n * 0.0009670257568359375
    r = r - n * 6.2783295730096264e-07
    z = r * r
    s = r * (1.0 + z * (-1.0 / 6 + z * (1.0 / 120 + z * (-1.0 / 5040 + z * (1.0 / 362880 - z * (1.0 / 39916800))))))
    c = 1.0 + z * (-0.5 + z * (1.0 / 24 + z * (-1.0 / 720 + z * (1.0 / 40320 + z * (-1.0 / 3628800 + z * (1.0 / 479001600))))))
    sin = 2.0 * s * c
    cos = 1.0 - 2.0 * s * s
    return re * cos - im * sin + pump, re * sin + im * cos


def real_form(re, im):
    top = jnp.concatenate([re, -im], axis=-1)
    low = jnp.concatenate([im, re], axis=-1)
    return jnp.concatenate([top, low], axis=-2)


def mode_tables():
    idx = np.arange(FACTOR)
    w = np.exp(2j * np.pi * ((idx[:, None] * idx[None, :]) % FACTOR) / FACTOR)
    tw = np.exp(2j * np.pi * (idx[:, None] * idx[None, :]) / M)
    k = FACTOR * idx[None, :] + idx[:, None]
    mu = np.where(k < M // 2, k, k - M) / M
    disp = np.exp(-1j * DISPERSION * mu * mu)

    def pair(a):
        return jnp.asarray(a.real, F32), jnp.asarray(a.imag, F32)

    wr, wi = pair(w)
    left = pair(tw.T[:, :, None])
    right = pair(disp[:, None, :])
    fr = wr * right[0] - wi * right[1]
    fi = wr * right[1] + wi * right[0]
    mr = fr * left[0] - fi * left[1]
    mi = fr * left[1] + fi * left[0]
    first = real_form(mr, mi)
    second = real_form(*pair(w / FACTOR))
    back_left = pair(np.conj(tw)[:, :, None] / FACTOR)
    br = wr * back_left[0] + wi * back_left[1]
    bi = wr * back_left[1] - wi * back_left[0]
    back = real_form(br, bi)
    inverse = real_form(*pair(np.conj(w)))
    middle = jnp.einsum("oab,bc->oac", first, inverse, precision=lax.Precision.HIGHEST)
    return first, second, back, middle


def lattice_operator(ext, zz, block, rows_total, cols_total, rows, width):
    er, ec = rows + 4, width + 4
    n = er * ec
    rr = (zz * rows - 2 + jnp.arange(er))[:, None]
    cc = (block * width - 2 + jnp.arange(ec))[None, :]
    live_r = (rr >= 0) & (rr < rows_total)
    live_c = (cc >= 0) & (cc < cols_total)
    a = 2.0 * math.pi / 64.0 * ext[:2]
    next_r = (rr + 1 >= 0) & (rr + 1 < rows_total)
    next_c = (cc + 1 >= 0) & (cc + 1 < cols_total)
    on0 = (live_r & next_r & live_c).astype(F32)
    on1 = (live_c & next_c & live_r).astype(F32)
    c0, s0 = ((on0 * jnp.cos(a[0])).reshape(n), (on0 * jnp.sin(a[0])).reshape(n))
    c1, s1 = ((on1 * jnp.cos(a[1])).reshape(n), (on1 * jnp.sin(a[1])).reshape(n))
    i = jnp.arange(n)[None, :]
    j = jnp.arange(n)[:, None]
    inner = (j % ec) != ec - 1
    inner_i = (i % ec) != ec - 1
    up = i == j + ec
    down = j == i + ec
    right = (i == j + 1) & inner
    left = (j == i + 1) & inner_i
    z = jnp.float32(0)
    hr = jnp.where(up, c0[:, None], z) + jnp.where(down, c0[None, :], z) + jnp.where(right, c1[:, None], z) + jnp.where(left, c1[None, :], z)
    hi = jnp.where(up, s0[:, None], z) - jnp.where(down, s0[None, :], z) + jnp.where(right, s1[:, None], z) - jnp.where(left, s1[None, :], z)

    def out_sites(h):
        return h.reshape(n, er, ec)[:, 2 : 2 + rows, 2 : 2 + width].reshape(n, rows * width)

    gr, gi = out_sites(hr), out_sites(hi)
    mm = functools.partial(jnp.matmul, precision=lax.Precision.HIGHEST)
    qr = mm(hr, gr) - mm(hi, gi)
    qi = mm(hr, gi) + mm(hi, gr)
    eye = out_sites((i == j).astype(F32))
    half = COUPLING * COUPLING / 2.0
    tr = eye + COUPLING * gi - half * qr
    ti = -COUPLING * gr - half * qi
    det = ext[2].reshape(n, 1)
    damp = math.exp(-LOSS_RATE)
    dr, di = damp * jnp.cos(det), -damp * jnp.sin(det)
    return (tr * dr - ti * di).reshape(er, ec, rows * width), (tr * di + ti * dr).reshape(er, ec, rows * width)


def operator_blocks(tr, ti, width):
    t = jnp.stack([jnp.stack([tr, ti], 2), jnp.stack([-ti, tr], 2)], 2)
    er = t.shape[0]
    kinds = er // 2
    main = t[:, 2 : 2 + width].reshape(kinds, 2, width, 2, 2, -1)
    main = main.transpose(0, 3, 1, 2, 4, 5).reshape(kinds, 2, 2 * width, 2, -1)
    edge = jnp.concatenate([t[:, :2], t[:, 2 + width :]], 1).reshape(kinds, 2, 4, 2, 2, -1)
    edge = edge.transpose(0, 3, 1, 2, 4, 5).reshape(kinds * 2 * 2 * 4, -1)
    return main, edge


def first_operator(main):
    zero = jnp.zeros_like(main)
    low = jnp.concatenate([main, zero], 2)
    high = jnp.concatenate([zero, main], 2)
    both = jnp.stack([low, high], 3)
    return both.reshape(both.shape[0] * 2 * LANES, -1)


def last_operator(main, edge):
    kinds = main.shape[0]
    half = LANES // 2
    m = main.reshape(kinds, 2, half, 2, 2, half)
    zero = jnp.zeros_like(m)
    h0 = jnp.concatenate([m, zero], -1)
    h1 = jnp.concatenate([zero, m], -1)
    own0 = jnp.concatenate([h0[1], h0[2]], 1).reshape(2 * LANES, -1)
    own1 = jnp.concatenate([h1[1], h1[2]], 1).reshape(2 * LANES, -1)
    up = jnp.concatenate([h0[0], h1[0]], 1).reshape(2 * LANES, -1)
    down = jnp.concatenate([h0[3], h1[3]], 1).reshape(2 * LANES, -1)
    e = edge.reshape(-1, 2, 2, half)
    ez = jnp.zeros_like(e)
    e0 = jnp.concatenate([e, ez], -1).reshape(edge.shape[0], -1)
    e1 = jnp.concatenate([ez, e], -1).reshape(edge.shape[0], -1)
    return jnp.concatenate([own0, own1, up, down], 0), jnp.stack([e0, e1])


def pack_kernel(x_ref, *o_refs):
    rows = [x_ref[0, h, :, r, :] for h in range(2) for r in range(2)]
    cols = rows[0].shape[1]
    w = LANES // 4
    for d in range(cols // w):
        got = jnp.concatenate([x[:, w * d : w * d + w] for x in rows], axis=1)
        n = got.shape[0] // len(o_refs)
        for i, o_ref in enumerate(o_refs):
            o_ref[d, 0] = got[n * i : n * (i + 1)]


def unpack_kernel(*refs):
    o_ref = refs[-1]
    w = LANES // 4
    count, _, n, _ = refs[0].shape
    for i, x_ref in enumerate(refs[:-1]):
        for h in range(2):
            for r in range(2):
                at = (2 * h + r) * w
                parts = [x_ref[d, 0, :, at : at + w] for d in range(count)]
                o_ref[0, h, n * i : n * (i + 1), r, :] = jnp.concatenate(parts, axis=1)


def wide(a):
    hi, lo = split(a)
    return jnp.concatenate([hi, lo, hi], axis=-1)


def dot_wide(a, b):
    hi, lo = split(b)
    return jnp.dot(a, jnp.concatenate([hi, hi, lo], axis=0), preferred_element_type=F32)


def first_kernel(own_ref, up_ref, down_ref, edge_ref, t_ref, te_ref, m_ref, o_ref):
    parts = [up_ref[0, 0], up_ref[0, 1], own_ref[0, 0, 0], own_ref[0, 0, 1]]
    parts += [own_ref[1, 0, 0], own_ref[1, 0, 1], down_ref[0, 0], down_ref[0, 1]]
    x = jnp.concatenate(parts, axis=1)
    n = x.shape[0]
    y = dot3(x, t_ref[...])
    e = edge_ref[0].T
    te = split(te_ref[...])
    for h in range(2):
        yh = y[:, 2 * LANES * h : 2 * LANES * (h + 1)] + dot3(e[n * h : n * (h + 1)], te)
        for o in range(n // FACTOR):
            rows = slice(FACTOR * o, FACTOR * (o + 1))
            b = jnp.concatenate([yh[rows, :LANES], yh[rows, LANES:]], axis=0)
            at = h * (n // FACTOR) + o
            o_ref[at] = dot_wide(wide(m_ref[at]), b).reshape(2, FACTOR, LANES)


def gather_rows(refs, at):
    return jnp.concatenate([r[:, c, at, :] for c in range(2) for r in refs], axis=0)


def middle_kernel(f_ref, back_ref, mid_ref, pump_ref, a_ref, w_ref, up_ref, down_ref, v_scratch, mid_scratch):
    f = wide(f_ref[...])
    pump = pump_ref[...]
    batch = 4

    def one(i, _):
        w = dot_wide(f, jnp.concatenate([gather_rows([a_ref], i * batch + j) for j in range(batch)], axis=1))
        for j in range(batch):
            wj = w[:, LANES * j : LANES * (j + 1)]
            re, im = kerr(wj[:FACTOR], wj[FACTOR:], pump)
            v = dot_wide(wide(back_ref[i * batch + j]), jnp.concatenate([re, im], axis=0))
            v_scratch[i * batch + j] = v.reshape(2, FACTOR, LANES)
        return 0

    lax.fori_loop(0, FACTOR // batch, one, 0)

    def two(i, _):
        for j in range(batch):
            o = i * batch + j
            v = dot_wide(wide(mid_ref[o]), gather_rows([v_scratch], o))
            mid_scratch[o] = v.reshape(2, FACTOR, LANES)
        return 0

    lax.fori_loop(0, FACTOR // batch, two, 0)

    eighth = w_ref.shape[2]
    size = batch // 2
    steps = eighth // size
    cut = LANES // 2

    def three(i, _):
        g, low = i // steps, (i % steps) * size
        s = [g * (2 * eighth) + h * eighth + low + j for h in range(2) for j in range(size)]
        w = dot_wide(f, jnp.concatenate([gather_rows([mid_scratch], at) for at in s], axis=1))
        for j in range(size):
            w0 = w[:, LANES * j : LANES * (j + 1)]
            w1 = w[:, LANES * (size + j) : LANES * (size + j + 1)]
            w_ref[g, 0, low + j] = w0.reshape(2, FACTOR, LANES)
            w_ref[g, 1, low + j] = w1.reshape(2, FACTOR, LANES)
            up = jnp.concatenate([w0[:, cut:], w1[:, cut:]], axis=1)
            down = jnp.concatenate([w0[:, :cut], w1[:, :cut]], axis=1)
            up_ref[g, low + j] = up.reshape(2, FACTOR, LANES)
            down_ref[g, low + j] = down.reshape(2, FACTOR, LANES)
        return 0

    lax.fori_loop(0, w_ref.shape[0] * steps, three, 0)


def last_kernel(tiles, w_ref, up_ref, down_ref, edge_ref, t_ref, te_ref, pump_ref, o_ref, up_buf, down_buf, stage, t_hi, t_lo, z_send, z_recv, x_send, x_recv):
    zz, yy, me = lax.axis_index("zz"), lax.axis_index("yy"), lax.axis_index("mode")
    groups, eighth = up_ref.shape[0], up_ref.shape[1]
    n = eighth * FACTOR
    cores = 2
    xs = groups // cores
    x, core = me // cores, me % cores
    has_before, has_after = zz > 0, zz < tiles - 1

    def group_at(k):
        return ((x + 1 + k // cores) % xs) * cores + (core + k + k // cores) % cores

    def peer(k, y):
        return {"yy": y, "mode": group_at(k)}

    barrier = pltpu.get_barrier_semaphore()

    def greet(where):
        pl.semaphore_signal(barrier, inc=1, device_id=where, device_id_type=MESH)

    for k in range(groups):
        greet(peer(k, 1 - yy))
        if k < groups - 1:
            greet(peer(k, yy))

    @pl.when(has_before)
    def _():
        greet({"zz": zz - 1})

    @pl.when(has_after)
    def _():
        greet({"zz": zz + 1})

    before = (zz + tiles - 1) // tiles
    after = 1 - (zz + 1) // tiles
    pl.semaphore_wait(barrier, 2 * groups - 1 + before + after)

    def upward(k):
        g = group_at(k)
        return pltpu.make_async_remote_copy(up_ref.at[g], up_buf.at[g], z_send.at[0, k], z_recv.at[0, k], device_id={"zz": zz + 1}, device_id_type=MESH)

    def downward(k):
        g = group_at(k)
        return pltpu.make_async_remote_copy(down_ref.at[g], down_buf.at[g], z_send.at[1, k], z_recv.at[1, k], device_id={"zz": zz - 1}, device_id_type=MESH)

    for k in range(groups):

        @pl.when(has_after)
        def _():
            upward(k).start()

        @pl.when(has_before)
        def _():
            downward(k).start()

    @pl.when(zz == 0)
    def _():
        up_buf[...] = jnp.zeros_like(up_buf)

    @pl.when(zz == tiles - 1)
    def _():
        down_buf[...] = jnp.zeros_like(down_buf)

    hi, lo = split(t_ref[...])
    t_hi[...] = hi
    t_lo[...] = lo
    mine = yy * groups + me

    def outward(k, y, at):
        return pltpu.make_async_remote_copy(stage.at[k, y], o_ref.at[mine], x_send.at[k, at], x_recv.at[k, at], device_id=peer(k, y), device_id_type=MESH)

    def one(k, _):
        g = group_at(k)

        @pl.when(has_before)
        def _():
            upward(k).wait_recv()

        @pl.when(has_after)
        def _():
            downward(k).wait_recv()

        parts = [w_ref[g, h, :, c].reshape(n, LANES) for h in range(2) for c in range(2)]
        parts += [ref[g, :, c].reshape(n, LANES) for ref in (up_buf, down_buf) for c in range(2)]
        y = dot3(jnp.concatenate(parts, axis=1), (t_hi[...], t_lo[...]))
        e = edge_ref[g].T
        for h in range(2):
            y = y + dot3(e[n * h : n * (h + 1)], te_ref[h])
        for side in range(2):
            re = y[:, LANES * side : LANES * (side + 1)]
            im = y[:, LANES * (2 + side) : LANES * (3 + side)]
            re, im = kerr(re, im, pump_ref[side : side + 1])
            stage[k, side, 0] = re
            stage[k, side, 1] = im
        outward(k, 1 - yy, 0).start()

        @pl.when(k < groups - 1)
        def _():
            outward(k, yy, 1).start()

        return 0

    lax.fori_loop(0, groups, one, 0)
    o_ref[mine] = stage[groups - 1, yy]
    for k in range(groups):
        outward(k, 1 - yy, 0).wait()
        if k < groups - 1:
            outward(k, yy, 1).wait()

        @pl.when(has_after)
        def _():
            upward(k).wait_send()

        @pl.when(has_before)
        def _():
            downward(k).wait_send()


def params():
    return pltpu.CompilerParams(vmem_limit_bytes=VMEM_LIMIT)


def whole(shape):
    return pl.BlockSpec(shape, lambda *_: (0,) * len(shape))


def body(tiles, groups, cycle_spectra, link_phase, pump_mask, detuning):
    modes, rows_in, cols = cycle_spectra.shape[1:]
    devices = 2 * groups
    width = cols // devices
    rows = 2 * rows_in
    half = modes // 2
    outer = modes // FACTOR
    zz = lax.axis_index("zz")
    block = lax.axis_index("yy") * groups + lax.axis_index("mode")
    up_perm = [(i, i + 1) for i in range(tiles - 1)]
    down_perm = [(i + 1, i) for i in range(tiles - 1)]

    def to_group(x):
        return lax.all_to_all(x, GROUP, split_axis=0, concat_axis=0, tiled=True)

    everyone = ("zz",) + GROUP
    cells = cycle_spectra.reshape(2, modes, rows_in, devices, width)
    none = jnp.zeros((2, modes, rows_in, 1, 2), F32)
    from_left = jnp.concatenate([none, cells[:, :, :, :-1, width - 2 :]], 3)
    from_right = jnp.concatenate([cells[:, :, :, 1:, :2], none], 3)
    rim = jnp.concatenate([from_left, from_right], 4).transpose(3, 0, 2, 4, 1)
    sites = jnp.concatenate([link_phase.astype(F32), detuning[None], pump_mask.astype(F32)[None]], 0)
    sites = jnp.pad(sites, ((0, 0), (0, 0), (2, 2)))
    sites = jnp.stack([sites[:, :, width * d : width * d + width + 4] for d in range(devices)])
    sites = jnp.pad(sites.reshape(devices, 4 * rows_in, width + 4), ((0, 0), (0, 0), (0, modes - width - 4)))
    edge_rows = 2 * rows_in * 4
    rim = jnp.concatenate([rim.reshape(devices, edge_rows, modes), sites], 1)
    rim = to_group(rim).reshape(2, groups, edge_rows + 4 * rows_in, modes)
    rim, cycle_spectra = lax.optimization_barrier((rim, cycle_spectra))
    packed = pl.pallas_call(
        pack_kernel,
        grid=(2,),
        in_specs=[pl.BlockSpec((1, 2, half, rows_in, cols), lambda c: (c, 0, 0, 0, 0))],
        out_specs=[pl.BlockSpec((devices, 1, half, LANES), lambda c: (0, c, 0, 0))],
        out_shape=[jax.ShapeDtypeStruct((devices, 2, half, LANES), F32)],
        compiler_params=params(),
    )(cycle_spectra.reshape(2, 2, half, rows_in, cols))[0]
    own = to_group(packed).reshape(2, groups, 2, half, LANES)
    rim_up = lax.ppermute(rim[1], "zz", up_perm)
    rim_down = lax.ppermute(rim[0], "zz", down_perm)
    kinds = [rim_up, rim[0], rim[1], rim_down]
    edge = jnp.concatenate([a[:, :edge_rows] for a in kinds], 1)
    ext = jnp.concatenate([a[0, edge_rows:, : width + 4].reshape(4, rows_in, width + 4) for a in kinds], 1)
    tr, ti = lattice_operator(ext, zz, block, tiles * rows, cols, rows, width)
    main, edge_op = operator_blocks(tr, ti, width)
    t_first = first_operator(main)
    t_last, edge_last = last_operator(main, edge_op)
    pump = PUMP_LEVEL * ext[3, 2 : 2 + rows, 2 : 2 + width]
    pump_flat = pump.reshape(1, rows * width)
    pump_half = pump.reshape(2, LANES // 2)
    pump_last = jnp.concatenate([pump_half, pump_half], 1)
    m_first, second, back, middle = mode_tables()
    up = lax.ppermute(own[1], "zz", up_perm)
    down = lax.ppermute(own[0], "zz", down_perm)

    full = (FACTOR, 2, FACTOR, LANES)
    stage = pl.pallas_call(
        first_kernel,
        grid=(groups,),
        in_specs=[
            pl.BlockSpec((2, 1, 2, half, LANES), lambda g: (0, g, 0, 0, 0)),
            pl.BlockSpec((1, 2, half, LANES), lambda g: (g, 0, 0, 0)),
            pl.BlockSpec((1, 2, half, LANES), lambda g: (g, 0, 0, 0)),
            pl.BlockSpec((1,) + edge.shape[1:], lambda g: (g, 0, 0)),
            whole(t_first.shape),
            whole(edge_op.shape),
            pl.BlockSpec((outer, LANES, LANES), lambda g: (g, 0, 0)),
        ],
        out_specs=pl.BlockSpec((outer, 2, FACTOR, LANES), lambda g: (g, 0, 0, 0)),
        out_shape=jax.ShapeDtypeStruct(full, F32),
        compiler_params=params(),
    )(own, up, down, edge, t_first, edge_op, m_first)

    eighth = outer // 2
    halo_shape = (groups, eighth, 2, FACTOR, LANES)
    wave, up, down = pl.pallas_call(
        middle_kernel,
        out_shape=[jax.ShapeDtypeStruct((groups, 2) + halo_shape[1:], F32)] + [jax.ShapeDtypeStruct(halo_shape, F32)] * 2,
        scratch_shapes=[pltpu.VMEM(full, F32), pltpu.VMEM(full, F32)],
        compiler_params=params(),
    )(second, back, middle, pump_flat, stage)

    rims = wave.reshape(FACTOR, 2, FACTOR, rows, width)
    sides = []
    for low, step in ((width - 2, 1), (0, -1)):
        cells = rims[..., low : low + 2].transpose(3, 1, 4, 0, 2).reshape(2, 2, 2, 2, M)
        took = []
        for source, turn in ((1, 1), (None, 0), (0, -1)):
            perm = []
            for at in range(tiles):
                for d in range(devices):
                    if 0 <= at + turn < tiles and 0 <= d + step < devices:
                        perm.append((at * devices + d, (at + turn) * devices + d + step))
            sent = cells if source is None else cells[source : source + 1]
            took.append(lax.ppermute(sent, everyone, perm))
        sides.append(jnp.concatenate(took, 0))
    edge = jnp.concatenate(sides, 3).transpose(0, 2, 1, 3, 4).reshape(-1, groups, modes).transpose(1, 0, 2)

    vmem = pl.BlockSpec(memory_space=pltpu.VMEM)
    arrived = pl.pallas_call(
        functools.partial(last_kernel, tiles),
        in_specs=[vmem] * 7,
        out_specs=vmem,
        out_shape=jax.ShapeDtypeStruct((devices, 2, half, LANES), F32),
        scratch_shapes=[
            pltpu.VMEM(halo_shape, F32),
            pltpu.VMEM(halo_shape, F32),
            pltpu.VMEM((groups, 2, 2, half, LANES), F32),
            pltpu.VMEM(t_last.shape, BF),
            pltpu.VMEM(t_last.shape, BF),
            pltpu.SemaphoreType.DMA((2, groups)),
            pltpu.SemaphoreType.DMA((2, groups)),
            pltpu.SemaphoreType.DMA((groups, 2)),
            pltpu.SemaphoreType.DMA((groups, 2)),
        ],
        compiler_params=pltpu.CompilerParams(vmem_limit_bytes=VMEM_LIMIT, collective_id=1, has_side_effects=True),
    )(wave, up, down, edge, t_last, edge_last, pump_last)
    samples = pl.pallas_call(
        unpack_kernel,
        grid=(2,),
        in_specs=[pl.BlockSpec((devices, 1, half, LANES), lambda c: (0, c, 0, 0))],
        out_specs=pl.BlockSpec((1, 2, half, rows_in, cols), lambda c: (c, 0, 0, 0, 0)),
        out_shape=jax.ShapeDtypeStruct((2, 2, half, rows_in, cols), F32),
        compiler_params=params(),
    )(arrived)
    return samples.reshape(2, modes, rows_in, cols)


def solution(mesh):
    names = mesh.axis_names
    tiles, groups = mesh.shape[names[0]], mesh.shape[names[1]]
    paired = Mesh(mesh.devices.reshape(tiles // 2, 2, groups), ("zz", "yy", "mode"))
    tile = ("zz", "yy")
    return jax.shard_map(
        functools.partial(body, tiles // 2, groups),
        mesh=paired,
        in_specs=(
            P(None, "mode", tile, None),
            P(None, tile, None),
            P(tile, None),
            P(tile, None),
        ),
        out_specs=P(None, "mode", tile, None),
        check_vma=False,
    )
```

```python
import functools
import math

import jax
import jax.numpy as jnp
import numpy as np
from jax import lax
from jax.experimental import pallas as pl
from jax.experimental.pallas import tpu as pltpu
from jax.sharding import Mesh, PartitionSpec as P

FACTOR = 64
M = FACTOR * FACTOR
LOSS_RATE = 0.05
DISPERSION = 8.0
KERR_GAIN = 0.5
PUMP_LEVEL = 1.0
COUPLING = 0.35

MESH = pl.DeviceIdType.MESH
GROUP = ("yy", "mode")
LANES = 128
BF = jnp.bfloat16
F32 = jnp.float32
VMEM_LIMIT = 56 * 1024 * 1024


def split(x):
    hi = x.astype(BF)
    return hi, (x - hi.astype(F32)).astype(BF)


def dot3(a, b):
    ah, al = a if isinstance(a, tuple) else split(a)
    bh, bl = b if isinstance(b, tuple) else split(b)
    one = functools.partial(jnp.dot, preferred_element_type=F32)
    return one(ah, bh) + (one(ah, bl) + one(al, bh))


def kerr(re, im, pump):
    half = (0.5 * KERR_GAIN) * (re * re + im * im)
    n = jnp.floor(half * (1.0 / math.pi) + 0.5)
    r = half - n * 3.140625
    r = r - n * 0.0009670257568359375
    r = r - n * 6.2783295730096264e-07
    z = r * r
    s = r * (1.0 + z * (-1.0 / 6 + z * (1.0 / 120 + z * (-1.0 / 5040 + z * (1.0 / 362880 - z * (1.0 / 39916800))))))
    c = 1.0 + z * (-0.5 + z * (1.0 / 24 + z * (-1.0 / 720 + z * (1.0 / 40320 + z * (-1.0 / 3628800 + z * (1.0 / 479001600))))))
    sin = 2.0 * s * c
    cos = 1.0 - 2.0 * s * s
    return re * cos - im * sin + pump, re * sin + im * cos


def real_form(re, im):
    top = jnp.concatenate([re, -im], axis=-1)
    low = jnp.concatenate([im, re], axis=-1)
    return jnp.concatenate([top, low], axis=-2)


def mode_tables():
    idx = np.arange(FACTOR)
    w = np.exp(2j * np.pi * ((idx[:, None] * idx[None, :]) % FACTOR) / FACTOR)
    tw = np.exp(2j * np.pi * (idx[:, None] * idx[None, :]) / M)
    k = FACTOR * idx[None, :] + idx[:, None]
    mu = np.where(k < M // 2, k, k - M) / M
    disp = np.exp(-1j * DISPERSION * mu * mu)

    def pair(a):
        return jnp.asarray(a.real, F32), jnp.asarray(a.imag, F32)

    wr, wi = pair(w)
    left = pair(tw.T[:, :, None])
    right = pair(disp[:, None, :])
    fr = wr * right[0] - wi * right[1]
    fi = wr * right[1] + wi * right[0]
    mr = fr * left[0] - fi * left[1]
    mi = fr * left[1] + fi * left[0]
    first = real_form(mr, mi)
    second = real_form(*pair(w / FACTOR))
    back_left = pair(np.conj(tw)[:, :, None] / FACTOR)
    br = wr * back_left[0] + wi * back_left[1]
    bi = wr * back_left[1] - wi * back_left[0]
    back = real_form(br, bi)
    inverse = real_form(*pair(np.conj(w)))
    middle = jnp.einsum("oab,bc->oac", first, inverse, precision=lax.Precision.HIGHEST)
    return first, second, back, middle


def lattice_operator(ext, zz, block, rows_total, cols_total, rows, width):
    er, ec = rows + 4, width + 4
    n = er * ec
    rr = (zz * rows - 2 + jnp.arange(er))[:, None]
    cc = (block * width - 2 + jnp.arange(ec))[None, :]
    live_r = (rr >= 0) & (rr < rows_total)
    live_c = (cc >= 0) & (cc < cols_total)
    a = 2.0 * math.pi / 64.0 * ext[:2]
    next_r = (rr + 1 >= 0) & (rr + 1 < rows_total)
    next_c = (cc + 1 >= 0) & (cc + 1 < cols_total)
    on0 = (live_r & next_r & live_c).astype(F32)
    on1 = (live_c & next_c & live_r).astype(F32)
    c0, s0 = ((on0 * jnp.cos(a[0])).reshape(n), (on0 * jnp.sin(a[0])).reshape(n))
    c1, s1 = ((on1 * jnp.cos(a[1])).reshape(n), (on1 * jnp.sin(a[1])).reshape(n))
    i = jnp.arange(n)[None, :]
    j = jnp.arange(n)[:, None]
    inner = (j % ec) != ec - 1
    inner_i = (i % ec) != ec - 1
    up = i == j + ec
    down = j == i + ec
    right = (i == j + 1) & inner
    left = (j == i + 1) & inner_i
    z = jnp.float32(0)
    hr = jnp.where(up, c0[:, None], z) + jnp.where(down, c0[None, :], z) + jnp.where(right, c1[:, None], z) + jnp.where(left, c1[None, :], z)
    hi = jnp.where(up, s0[:, None], z) - jnp.where(down, s0[None, :], z) + jnp.where(right, s1[:, None], z) - jnp.where(left, s1[None, :], z)

    def out_sites(h):
        return h.reshape(n, er, ec)[:, 2 : 2 + rows, 2 : 2 + width].reshape(n, rows * width)

    gr, gi = out_sites(hr), out_sites(hi)
    mm = functools.partial(jnp.matmul, precision=lax.Precision.HIGHEST)
    qr = mm(hr, gr) - mm(hi, gi)
    qi = mm(hr, gi) + mm(hi, gr)
    eye = out_sites((i == j).astype(F32))
    half = COUPLING * COUPLING / 2.0
    tr = eye + COUPLING * gi - half * qr
    ti = -COUPLING * gr - half * qi
    det = ext[2].reshape(n, 1)
    damp = math.exp(-LOSS_RATE)
    dr, di = damp * jnp.cos(det), -damp * jnp.sin(det)
    return (tr * dr - ti * di).reshape(er, ec, rows * width), (tr * di + ti * dr).reshape(er, ec, rows * width)


def operator_blocks(tr, ti, width):
    t = jnp.stack([jnp.stack([tr, ti], 2), jnp.stack([-ti, tr], 2)], 2)
    er = t.shape[0]
    kinds = er // 2
    main = t[:, 2 : 2 + width].reshape(kinds, 2, width, 2, 2, -1)
    main = main.transpose(0, 3, 1, 2, 4, 5).reshape(kinds, 2, 2 * width, 2, -1)
    edge = jnp.concatenate([t[:, :2], t[:, 2 + width :]], 1).reshape(kinds, 2, 4, 2, 2, -1)
    edge = edge.transpose(0, 3, 1, 2, 4, 5).reshape(kinds * 2 * 2 * 4, -1)
    return main, edge


def first_operator(main):
    zero = jnp.zeros_like(main)
    low = jnp.concatenate([main, zero], 2)
    high = jnp.concatenate([zero, main], 2)
    both = jnp.stack([low, high], 3)
    return both.reshape(both.shape[0] * 2 * LANES, -1)


def last_operator(main, edge):
    kinds = main.shape[0]
    half = LANES // 2
    m = main.reshape(kinds, 2, half, 2, 2, half)
    zero = jnp.zeros_like(m)
    h0 = jnp.concatenate([m, zero], -1)
    h1 = jnp.concatenate([zero, m], -1)
    own0 = jnp.concatenate([h0[1], h0[2]], 1).reshape(2 * LANES, -1)
    own1 = jnp.concatenate([h1[1], h1[2]], 1).reshape(2 * LANES, -1)
    up = jnp.concatenate([h0[0], h1[0]], 1).reshape(2 * LANES, -1)
    down = jnp.concatenate([h0[3], h1[3]], 1).reshape(2 * LANES, -1)
    e = edge.reshape(-1, 2, 2, half)
    ez = jnp.zeros_like(e)
    e0 = jnp.concatenate([e, ez], -1).reshape(edge.shape[0], -1)
    e1 = jnp.concatenate([ez, e], -1).reshape(edge.shape[0], -1)
    return jnp.concatenate([own0, own1, up, down], 0), jnp.stack([e0, e1])


def pack_kernel(x_ref, *o_refs):
    rows = [x_ref[0, h, :, r, :] for h in range(2) for r in range(2)]
    cols = rows[0].shape[1]
    w = LANES // 4
    for d in range(cols // w):
        got = jnp.concatenate([x[:, w * d : w * d + w] for x in rows], axis=1)
        n = got.shape[0] // len(o_refs)
        for i, o_ref in enumerate(o_refs):
            o_ref[d, 0] = got[n * i : n * (i + 1)]


def unpack_kernel(*refs):
    o_ref = refs[-1]
    w = LANES // 4
    count, _, n, _ = refs[0].shape
    for i, x_ref in enumerate(refs[:-1]):
        for h in range(2):
            for r in range(2):
                at = (2 * h + r) * w
                parts = [x_ref[d, 0, :, at : at + w] for d in range(count)]
                o_ref[0, h, n * i : n * (i + 1), r, :] = jnp.concatenate(parts, axis=1)


def wide(a):
    hi, lo = split(a)
    return jnp.concatenate([hi, lo, hi], axis=-1)


def dot_wide(a, b):
    hi, lo = split(b)
    return jnp.dot(a, jnp.concatenate([hi, hi, lo], axis=0), preferred_element_type=F32)


def first_kernel(tiles, own_ref, edge_ref, t_ref, te_ref, m_ref, o_ref, up_buf, down_buf, t_hi, t_lo, z_send, z_recv):
    zz = lax.axis_index("zz")
    groups, _, n, _ = up_buf.shape
    has_before, has_after = zz > 0, zz < tiles - 1
    barrier = pltpu.get_barrier_semaphore()

    @pl.when(has_before)
    def _():
        pl.semaphore_signal(barrier, inc=1, device_id={"zz": zz - 1}, device_id_type=MESH)

    @pl.when(has_after)
    def _():
        pl.semaphore_signal(barrier, inc=1, device_id={"zz": zz + 1}, device_id_type=MESH)

    before = (zz + tiles - 1) // tiles
    after = 1 - (zz + 1) // tiles
    pl.semaphore_wait(barrier, before + after)

    def upward(g):
        return pltpu.make_async_remote_copy(own_ref.at[1, g], up_buf.at[g], z_send.at[0, g], z_recv.at[0, g], device_id={"zz": zz + 1}, device_id_type=MESH)

    def downward(g):
        return pltpu.make_async_remote_copy(own_ref.at[0, g], down_buf.at[g], z_send.at[1, g], z_recv.at[1, g], device_id={"zz": zz - 1}, device_id_type=MESH)

    for g in range(groups):

        @pl.when(has_after)
        def _():
            upward(g).start()

        @pl.when(has_before)
        def _():
            downward(g).start()

    @pl.when(zz == 0)
    def _():
        up_buf[...] = jnp.zeros_like(up_buf)

    @pl.when(zz == tiles - 1)
    def _():
        down_buf[...] = jnp.zeros_like(down_buf)

    hi, lo = split(t_ref[...])
    t_hi[...] = hi
    t_lo[...] = lo
    each = n // FACTOR

    def one(g, _):
        @pl.when(has_before)
        def _():
            upward(g).wait_recv()

        @pl.when(has_after)
        def _():
            downward(g).wait_recv()

        parts = [up_buf[g, c] for c in range(2)] + [own_ref[y, g, c] for y in range(2) for c in range(2)]
        parts += [down_buf[g, c] for c in range(2)]
        y = dot3(jnp.concatenate(parts, axis=1), (t_hi[...], t_lo[...]))
        e = edge_ref[g].T
        te = split(te_ref[...])
        for h in range(2):
            yh = y[:, 2 * LANES * h : 2 * LANES * (h + 1)] + dot3(e[n * h : n * (h + 1)], te)
            for o in range(each):
                rows = slice(FACTOR * o, FACTOR * (o + 1))
                b = jnp.concatenate([yh[rows, :LANES], yh[rows, LANES:]], axis=0)
                at = g * (2 * each) + h * each + o
                o_ref[at] = dot_wide(wide(m_ref[at]), b).reshape(2, FACTOR, LANES)
        return 0

    lax.fori_loop(0, groups, one, 0)
    for g in range(groups):

        @pl.when(has_after)
        def _():
            upward(g).wait_send()

        @pl.when(has_before)
        def _():
            downward(g).wait_send()


def gather_rows(refs, at):
    return jnp.concatenate([r[:, c, at, :] for c in range(2) for r in refs], axis=0)


def middle_kernel(f_ref, back_ref, mid_ref, pump_ref, a_ref, w_ref, up_ref, down_ref, v_scratch, mid_scratch):
    f = wide(f_ref[...])
    pump = pump_ref[...]
    batch = 4

    def one(i, _):
        w = dot_wide(f, jnp.concatenate([gather_rows([a_ref], i * batch + j) for j in range(batch)], axis=1))
        for j in range(batch):
            wj = w[:, LANES * j : LANES * (j + 1)]
            re, im = kerr(wj[:FACTOR], wj[FACTOR:], pump)
            v = dot_wide(wide(back_ref[i * batch + j]), jnp.concatenate([re, im], axis=0))
            v_scratch[i * batch + j] = v.reshape(2, FACTOR, LANES)
        return 0

    lax.fori_loop(0, FACTOR // batch, one, 0)

    def two(i, _):
        for j in range(batch):
            o = i * batch + j
            v = dot_wide(wide(mid_ref[o]), gather_rows([v_scratch], o))
            mid_scratch[o] = v.reshape(2, FACTOR, LANES)
        return 0

    lax.fori_loop(0, FACTOR // batch, two, 0)

    eighth = w_ref.shape[2]
    size = batch // 2
    steps = eighth // size
    cut = LANES // 2

    def three(i, _):
        g, low = i // steps, (i % steps) * size
        s = [g * (2 * eighth) + h * eighth + low + j for h in range(2) for j in range(size)]
        w = dot_wide(f, jnp.concatenate([gather_rows([mid_scratch], at) for at in s], axis=1))
        for j in range(size):
            w0 = w[:, LANES * j : LANES * (j + 1)]
            w1 = w[:, LANES * (size + j) : LANES * (size + j + 1)]
            w_ref[g, 0, low + j] = w0.reshape(2, FACTOR, LANES)
            w_ref[g, 1, low + j] = w1.reshape(2, FACTOR, LANES)
            up = jnp.concatenate([w0[:, cut:], w1[:, cut:]], axis=1)
            down = jnp.concatenate([w0[:, :cut], w1[:, :cut]], axis=1)
            up_ref[g, low + j] = up.reshape(2, FACTOR, LANES)
            down_ref[g, low + j] = down.reshape(2, FACTOR, LANES)
        return 0

    lax.fori_loop(0, w_ref.shape[0] * steps, three, 0)


def last_kernel(tiles, w_ref, up_ref, down_ref, edge_ref, t_ref, te_ref, pump_ref, o_ref, up_buf, down_buf, stage, t_hi, t_lo, z_send, z_recv, x_send, x_recv):
    zz, yy, me = lax.axis_index("zz"), lax.axis_index("yy"), lax.axis_index("mode")
    groups, eighth = up_ref.shape[0], up_ref.shape[1]
    n = eighth * FACTOR
    cores = 2
    xs = groups // cores
    x, core = me // cores, me % cores
    has_before, has_after = zz > 0, zz < tiles - 1

    def group_at(k):
        return ((x + 1 + k // cores) % xs) * cores + (core + k + k // cores) % cores

    def peer(k, y):
        return {"yy": y, "mode": group_at(k)}

    barrier = pltpu.get_barrier_semaphore()

    def greet(where):
        pl.semaphore_signal(barrier, inc=1, device_id=where, device_id_type=MESH)

    for k in range(groups):
        greet(peer(k, 1 - yy))
        if k < groups - 1:
            greet(peer(k, yy))

    @pl.when(has_before)
    def _():
        greet({"zz": zz - 1})

    @pl.when(has_after)
    def _():
        greet({"zz": zz + 1})

    before = (zz + tiles - 1) // tiles
    after = 1 - (zz + 1) // tiles
    pl.semaphore_wait(barrier, 2 * groups - 1 + before + after)

    def upward(k):
        g = group_at(k)
        return pltpu.make_async_remote_copy(up_ref.at[g], up_buf.at[g], z_send.at[0, k], z_recv.at[0, k], device_id={"zz": zz + 1}, device_id_type=MESH)

    def downward(k):
        g = group_at(k)
        return pltpu.make_async_remote_copy(down_ref.at[g], down_buf.at[g], z_send.at[1, k], z_recv.at[1, k], device_id={"zz": zz - 1}, device_id_type=MESH)

    for k in range(groups):

        @pl.when(has_after)
        def _():
            upward(k).start()

        @pl.when(has_before)
        def _():
            downward(k).start()

    @pl.when(zz == 0)
    def _():
        up_buf[...] = jnp.zeros_like(up_buf)

    @pl.when(zz == tiles - 1)
    def _():
        down_buf[...] = jnp.zeros_like(down_buf)

    hi, lo = split(t_ref[...])
    t_hi[...] = hi
    t_lo[...] = lo
    mine = yy * groups + me

    def outward(k, y, at):
        return pltpu.make_async_remote_copy(stage.at[k, y], o_ref.at[mine], x_send.at[k, at], x_recv.at[k, at], device_id=peer(k, y), device_id_type=MESH)

    def one(k, _):
        g = group_at(k)

        @pl.when(has_before)
        def _():
            upward(k).wait_recv()

        @pl.when(has_after)
        def _():
            downward(k).wait_recv()

        parts = [w_ref[g, h, :, c].reshape(n, LANES) for h in range(2) for c in range(2)]
        parts += [ref[g, :, c].reshape(n, LANES) for ref in (up_buf, down_buf) for c in range(2)]
        y = dot3(jnp.concatenate(parts, axis=1), (t_hi[...], t_lo[...]))
        e = edge_ref[g].T
        for h in range(2):
            y = y + dot3(e[n * h : n * (h + 1)], te_ref[h])
        for side in range(2):
            re = y[:, LANES * side : LANES * (side + 1)]
            im = y[:, LANES * (2 + side) : LANES * (3 + side)]
            re, im = kerr(re, im, pump_ref[side : side + 1])
            stage[k, side, 0] = re
            stage[k, side, 1] = im
        outward(k, 1 - yy, 0).start()

        @pl.when(k < groups - 1)
        def _():
            outward(k, yy, 1).start()

        return 0

    lax.fori_loop(0, groups, one, 0)
    o_ref[mine] = stage[groups - 1, yy]
    for k in range(groups):
        outward(k, 1 - yy, 0).wait()
        if k < groups - 1:
            outward(k, yy, 1).wait()

        @pl.when(has_after)
        def _():
            upward(k).wait_send()

        @pl.when(has_before)
        def _():
            downward(k).wait_send()


def params():
    return pltpu.CompilerParams(vmem_limit_bytes=VMEM_LIMIT)


def whole(shape):
    return pl.BlockSpec(shape, lambda *_: (0,) * len(shape))


def body(tiles, groups, cycle_spectra, link_phase, pump_mask, detuning):
    modes, rows_in, cols = cycle_spectra.shape[1:]
    devices = 2 * groups
    width = cols // devices
    rows = 2 * rows_in
    half = modes // 2
    outer = modes // FACTOR
    zz = lax.axis_index("zz")
    block = lax.axis_index("yy") * groups + lax.axis_index("mode")
    up_perm = [(i, i + 1) for i in range(tiles - 1)]
    down_perm = [(i + 1, i) for i in range(tiles - 1)]

    def to_group(x):
        return lax.all_to_all(x, GROUP, split_axis=0, concat_axis=0, tiled=True)

    everyone = ("zz",) + GROUP
    cells = cycle_spectra.reshape(2, modes, rows_in, devices, width)
    none = jnp.zeros((2, modes, rows_in, 1, 2), F32)
    from_left = jnp.concatenate([none, cells[:, :, :, :-1, width - 2 :]], 3)
    from_right = jnp.concatenate([cells[:, :, :, 1:, :2], none], 3)
    rim = jnp.concatenate([from_left, from_right], 4).transpose(3, 0, 2, 4, 1)
    sites = jnp.concatenate([link_phase.astype(F32), detuning[None], pump_mask.astype(F32)[None]], 0)
    sites = jnp.pad(sites, ((0, 0), (0, 0), (2, 2)))
    sites = jnp.stack([sites[:, :, width * d : width * d + width + 4] for d in range(devices)])
    sites = jnp.pad(sites.reshape(devices, 4 * rows_in, width + 4), ((0, 0), (0, 0), (0, modes - width - 4)))
    edge_rows = 2 * rows_in * 4
    rim = jnp.concatenate([rim.reshape(devices, edge_rows, modes), sites], 1)
    rim = to_group(rim).reshape(2, groups, edge_rows + 4 * rows_in, modes)
    rim, cycle_spectra = lax.optimization_barrier((rim, cycle_spectra))
    packed = pl.pallas_call(
        pack_kernel,
        grid=(2,),
        in_specs=[pl.BlockSpec((1, 2, half, rows_in, cols), lambda c: (c, 0, 0, 0, 0))],
        out_specs=[pl.BlockSpec((devices, 1, half, LANES), lambda c: (0, c, 0, 0))],
        out_shape=[jax.ShapeDtypeStruct((devices, 2, half, LANES), F32)],
        compiler_params=params(),
    )(cycle_spectra.reshape(2, 2, half, rows_in, cols))[0]
    own = to_group(packed).reshape(2, groups, 2, half, LANES)
    rim_up = lax.ppermute(rim[1], "zz", up_perm)
    rim_down = lax.ppermute(rim[0], "zz", down_perm)
    kinds = [rim_up, rim[0], rim[1], rim_down]
    edge = jnp.concatenate([a[:, :edge_rows] for a in kinds], 1)
    ext = jnp.concatenate([a[0, edge_rows:, : width + 4].reshape(4, rows_in, width + 4) for a in kinds], 1)
    tr, ti = lattice_operator(ext, zz, block, tiles * rows, cols, rows, width)
    main, edge_op = operator_blocks(tr, ti, width)
    t_first = first_operator(main)
    t_last, edge_last = last_operator(main, edge_op)
    pump = PUMP_LEVEL * ext[3, 2 : 2 + rows, 2 : 2 + width]
    pump_flat = pump.reshape(1, rows * width)
    pump_half = pump.reshape(2, LANES // 2)
    pump_last = jnp.concatenate([pump_half, pump_half], 1)
    m_first, second, back, middle = mode_tables()
    full = (FACTOR, 2, FACTOR, LANES)
    vmem = pl.BlockSpec(memory_space=pltpu.VMEM)
    stage = pl.pallas_call(
        functools.partial(first_kernel, tiles),
        in_specs=[vmem] * 5,
        out_specs=vmem,
        out_shape=jax.ShapeDtypeStruct(full, F32),
        scratch_shapes=[
            pltpu.VMEM(own.shape[1:], F32),
            pltpu.VMEM(own.shape[1:], F32),
            pltpu.VMEM(t_first.shape, BF),
            pltpu.VMEM(t_first.shape, BF),
            pltpu.SemaphoreType.DMA((2, groups)),
            pltpu.SemaphoreType.DMA((2, groups)),
        ],
        compiler_params=pltpu.CompilerParams(vmem_limit_bytes=VMEM_LIMIT, collective_id=2, has_side_effects=True),
    )(own, edge, t_first, edge_op, m_first)

    eighth = outer // 2
    halo_shape = (groups, eighth, 2, FACTOR, LANES)
    wave, up, down = pl.pallas_call(
        middle_kernel,
        out_shape=[jax.ShapeDtypeStruct((groups, 2) + halo_shape[1:], F32)] + [jax.ShapeDtypeStruct(halo_shape, F32)] * 2,
        scratch_shapes=[pltpu.VMEM(full, F32), pltpu.VMEM(full, F32)],
        compiler_params=params(),
    )(second, back, middle, pump_flat, stage)

    rims = wave.reshape(FACTOR, 2, FACTOR, rows, width)
    sides = []
    for low, step in ((width - 2, 1), (0, -1)):
        cells = rims[..., low : low + 2].transpose(3, 1, 4, 0, 2).reshape(2, 2, 2, 2, M)
        took = []
        for source, turn in ((1, 1), (None, 0), (0, -1)):
            perm = []
            for at in range(tiles):
                for d in range(devices):
                    if 0 <= at + turn < tiles and 0 <= d + step < devices:
                        perm.append((at * devices + d, (at + turn) * devices + d + step))
            sent = cells if source is None else cells[source : source + 1]
            took.append(lax.ppermute(sent, everyone, perm))
        sides.append(jnp.concatenate(took, 0))
    edge = jnp.concatenate(sides, 3).transpose(0, 2, 1, 3, 4).reshape(-1, groups, modes).transpose(1, 0, 2)

    arrived = pl.pallas_call(
        functools.partial(last_kernel, tiles),
        in_specs=[vmem] * 7,
        out_specs=vmem,
        out_shape=jax.ShapeDtypeStruct((devices, 2, half, LANES), F32),
        scratch_shapes=[
            pltpu.VMEM(halo_shape, F32),
            pltpu.VMEM(halo_shape, F32),
            pltpu.VMEM((groups, 2, 2, half, LANES), F32),
            pltpu.VMEM(t_last.shape, BF),
            pltpu.VMEM(t_last.shape, BF),
            pltpu.SemaphoreType.DMA((2, groups)),
            pltpu.SemaphoreType.DMA((2, groups)),
            pltpu.SemaphoreType.DMA((groups, 2)),
            pltpu.SemaphoreType.DMA((groups, 2)),
        ],
        compiler_params=pltpu.CompilerParams(vmem_limit_bytes=VMEM_LIMIT, collective_id=1, has_side_effects=True),
    )(wave, up, down, edge, t_last, edge_last, pump_last)
    samples = pl.pallas_call(
        unpack_kernel,
        grid=(2,),
        in_specs=[pl.BlockSpec((devices, 1, half, LANES), lambda c: (0, c, 0, 0))],
        out_specs=pl.BlockSpec((1, 2, half, rows_in, cols), lambda c: (c, 0, 0, 0, 0)),
        out_shape=jax.ShapeDtypeStruct((2, 2, half, rows_in, cols), F32),
        compiler_params=params(),
    )(arrived)
    return samples.reshape(2, modes, rows_in, cols)


def solution(mesh):
    names = mesh.axis_names
    tiles, groups = mesh.shape[names[0]], mesh.shape[names[1]]
    paired = Mesh(mesh.devices.reshape(tiles // 2, 2, groups), ("zz", "yy", "mode"))
    tile = ("zz", "yy")
    return jax.shard_map(
        functools.partial(body, tiles // 2, groups),
        mesh=paired,
        in_specs=(
            P(None, "mode", tile, None),
            P(None, tile, None),
            P(tile, None),
            P(tile, None),
        ),
        out_specs=P(None, "mode", tile, None),
        check_vma=False,
    )
```

```python
import functools
import math

import jax
import jax.numpy as jnp
import numpy as np
from jax import lax
from jax.experimental import pallas as pl
from jax.experimental.pallas import tpu as pltpu
from jax.sharding import Mesh, PartitionSpec as P

FACTOR = 64
M = FACTOR * FACTOR
LOSS_RATE = 0.05
DISPERSION = 8.0
KERR_GAIN = 0.5
PUMP_LEVEL = 1.0
COUPLING = 0.35

MESH = pl.DeviceIdType.MESH
GROUP = ("yy", "mode")
LANES = 128
BF = jnp.bfloat16
F32 = jnp.float32
VMEM_LIMIT = 56 * 1024 * 1024


def split(x):
    hi = x.astype(BF)
    return hi, (x - hi.astype(F32)).astype(BF)


def dot3(a, b):
    ah, al = a if isinstance(a, tuple) else split(a)
    bh, bl = b if isinstance(b, tuple) else split(b)
    one = functools.partial(jnp.dot, preferred_element_type=F32)
    return one(ah, bh) + (one(ah, bl) + one(al, bh))


def kerr(re, im, pump):
    half = (0.5 * KERR_GAIN) * (re * re + im * im)
    n = jnp.floor(half * (1.0 / math.pi) + 0.5)
    r = half - n * 3.140625
    r = r - n * 0.0009670257568359375
    r = r - n * 6.2783295730096264e-07
    z = r * r
    s = r * (1.0 + z * (-1.0 / 6 + z * (1.0 / 120 + z * (-1.0 / 5040 + z * (1.0 / 362880 - z * (1.0 / 39916800))))))
    c = 1.0 + z * (-0.5 + z * (1.0 / 24 + z * (-1.0 / 720 + z * (1.0 / 40320 + z * (-1.0 / 3628800 + z * (1.0 / 479001600))))))
    sin = 2.0 * s * c
    cos = 1.0 - 2.0 * s * s
    return re * cos - im * sin + pump, re * sin + im * cos


def real_form(re, im):
    top = jnp.concatenate([re, -im], axis=-1)
    low = jnp.concatenate([im, re], axis=-1)
    return jnp.concatenate([top, low], axis=-2)


def mode_tables():
    idx = np.arange(FACTOR)
    w = np.exp(2j * np.pi * ((idx[:, None] * idx[None, :]) % FACTOR) / FACTOR)
    tw = np.exp(2j * np.pi * (idx[:, None] * idx[None, :]) / M)
    k = FACTOR * idx[None, :] + idx[:, None]
    mu = np.where(k < M // 2, k, k - M) / M
    disp = np.exp(-1j * DISPERSION * mu * mu)

    def pair(a):
        return jnp.asarray(a.real, F32), jnp.asarray(a.imag, F32)

    wr, wi = pair(w)
    left = pair(tw.T[:, :, None])
    right = pair(disp[:, None, :])
    fr = wr * right[0] - wi * right[1]
    fi = wr * right[1] + wi * right[0]
    mr = fr * left[0] - fi * left[1]
    mi = fr * left[1] + fi * left[0]
    first = real_form(mr, mi)
    second = real_form(*pair(w / FACTOR))
    back_left = pair(np.conj(tw)[:, :, None] / FACTOR)
    br = wr * back_left[0] + wi * back_left[1]
    bi = wr * back_left[1] - wi * back_left[0]
    back = real_form(br, bi)
    inverse = real_form(*pair(np.conj(w)))
    middle = jnp.einsum("oab,bc->oac", first, inverse, precision=lax.Precision.HIGHEST)
    return first, second, back, middle


def lattice_operator(ext, zz, block, rows_total, cols_total, rows, width):
    er, ec = rows + 4, width + 4
    n = er * ec
    rr = (zz * rows - 2 + jnp.arange(er))[:, None]
    cc = (block * width - 2 + jnp.arange(ec))[None, :]
    live_r = (rr >= 0) & (rr < rows_total)
    live_c = (cc >= 0) & (cc < cols_total)
    a = 2.0 * math.pi / 64.0 * ext[:2]
    next_r = (rr + 1 >= 0) & (rr + 1 < rows_total)
    next_c = (cc + 1 >= 0) & (cc + 1 < cols_total)
    on0 = (live_r & next_r & live_c).astype(F32)
    on1 = (live_c & next_c & live_r).astype(F32)
    c0, s0 = ((on0 * jnp.cos(a[0])).reshape(n), (on0 * jnp.sin(a[0])).reshape(n))
    c1, s1 = ((on1 * jnp.cos(a[1])).reshape(n), (on1 * jnp.sin(a[1])).reshape(n))
    i = jnp.arange(n)[None, :]
    j = jnp.arange(n)[:, None]
    inner = (j % ec) != ec - 1
    inner_i = (i % ec) != ec - 1
    up = i == j + ec
    down = j == i + ec
    right = (i == j + 1) & inner
    left = (j == i + 1) & inner_i
    z = jnp.float32(0)
    hr = jnp.where(up, c0[:, None], z) + jnp.where(down, c0[None, :], z) + jnp.where(right, c1[:, None], z) + jnp.where(left, c1[None, :], z)
    hi = jnp.where(up, s0[:, None], z) - jnp.where(down, s0[None, :], z) + jnp.where(right, s1[:, None], z) - jnp.where(left, s1[None, :], z)

    def out_sites(h):
        return h.reshape(n, er, ec)[:, 2 : 2 + rows, 2 : 2 + width].reshape(n, rows * width)

    gr, gi = out_sites(hr), out_sites(hi)
    mm = functools.partial(jnp.matmul, precision=lax.Precision.HIGHEST)
    qr = mm(hr, gr) - mm(hi, gi)
    qi = mm(hr, gi) + mm(hi, gr)
    eye = out_sites((i == j).astype(F32))
    half = COUPLING * COUPLING / 2.0
    tr = eye + COUPLING * gi - half * qr
    ti = -COUPLING * gr - half * qi
    det = ext[2].reshape(n, 1)
    damp = math.exp(-LOSS_RATE)
    dr, di = damp * jnp.cos(det), -damp * jnp.sin(det)
    return (tr * dr - ti * di).reshape(er, ec, rows * width), (tr * di + ti * dr).reshape(er, ec, rows * width)


def operator_blocks(tr, ti, width):
    t = jnp.stack([jnp.stack([tr, ti], 2), jnp.stack([-ti, tr], 2)], 2)
    er = t.shape[0]
    kinds = er // 2
    main = t[:, 2 : 2 + width].reshape(kinds, 2, width, 2, 2, -1)
    main = main.transpose(0, 3, 1, 2, 4, 5).reshape(kinds, 2, 2 * width, 2, -1)
    edge = jnp.concatenate([t[:, :2], t[:, 2 + width :]], 1).reshape(kinds, 2, 4, 2, 2, -1)
    edge = edge.transpose(0, 3, 1, 2, 4, 5).reshape(kinds * 2 * 2 * 4, -1)
    return main, edge


def first_operator(main):
    zero = jnp.zeros_like(main)
    low = jnp.concatenate([main, zero], 2)
    high = jnp.concatenate([zero, main], 2)
    both = jnp.stack([low, high], 3)
    return both.reshape(both.shape[0] * 2 * LANES, -1)


def last_operator(main, edge):
    kinds = main.shape[0]
    half = LANES // 2
    m = main.reshape(kinds, 2, half, 2, 2, half)
    zero = jnp.zeros_like(m)
    h0 = jnp.concatenate([m, zero], -1)
    h1 = jnp.concatenate([zero, m], -1)
    own0 = jnp.concatenate([h0[1], h0[2]], 1).reshape(2 * LANES, -1)
    own1 = jnp.concatenate([h1[1], h1[2]], 1).reshape(2 * LANES, -1)
    up = jnp.concatenate([h0[0], h1[0]], 1).reshape(2 * LANES, -1)
    down = jnp.concatenate([h0[3], h1[3]], 1).reshape(2 * LANES, -1)
    e = edge.reshape(-1, 2, 2, half)
    ez = jnp.zeros_like(e)
    e0 = jnp.concatenate([e, ez], -1).reshape(edge.shape[0], -1)
    e1 = jnp.concatenate([ez, e], -1).reshape(edge.shape[0], -1)
    return jnp.concatenate([own0, own1, up, down], 0), jnp.stack([e0, e1])


def pack_kernel(x_ref, *o_refs):
    rows = [x_ref[0, h, :, r, :] for h in range(2) for r in range(2)]
    cols = rows[0].shape[1]
    w = LANES // 4
    for d in range(cols // w):
        got = jnp.concatenate([x[:, w * d : w * d + w] for x in rows], axis=1)
        n = got.shape[0] // len(o_refs)
        for i, o_ref in enumerate(o_refs):
            o_ref[d, 0] = got[n * i : n * (i + 1)]


def unpack_kernel(*refs):
    o_ref = refs[-1]
    w = LANES // 4
    count, _, n, _ = refs[0].shape
    for i, x_ref in enumerate(refs[:-1]):
        for h in range(2):
            for r in range(2):
                at = (2 * h + r) * w
                parts = [x_ref[d, 0, :, at : at + w] for d in range(count)]
                o_ref[0, h, n * i : n * (i + 1), r, :] = jnp.concatenate(parts, axis=1)


def wide(a):
    hi, lo = split(a)
    return jnp.concatenate([hi, lo, hi], axis=-1)


def dot_wide(a, b):
    hi, lo = split(b)
    return jnp.dot(a, jnp.concatenate([hi, hi, lo], axis=0), preferred_element_type=F32)


def first_kernel(own_ref, up_ref, down_ref, edge_ref, t_ref, te_ref, m_ref, o_ref):
    parts = [up_ref[0, 0], up_ref[0, 1], own_ref[0, 0, 0], own_ref[0, 0, 1]]
    parts += [own_ref[1, 0, 0], own_ref[1, 0, 1], down_ref[0, 0], down_ref[0, 1]]
    x = jnp.concatenate(parts, axis=1)
    n = x.shape[0]
    y = dot3(x, t_ref[...])
    e = edge_ref[0].T
    te = split(te_ref[...])
    for h in range(2):
        yh = y[:, 2 * LANES * h : 2 * LANES * (h + 1)] + dot3(e[n * h : n * (h + 1)], te)
        for o in range(n // FACTOR):
            rows = slice(FACTOR * o, FACTOR * (o + 1))
            b = jnp.concatenate([yh[rows, :LANES], yh[rows, LANES:]], axis=0)
            at = h * (n // FACTOR) + o
            o_ref[at] = dot_wide(wide(m_ref[at]), b).reshape(2, FACTOR, LANES)


def gather_rows(refs, at):
    return jnp.concatenate([r[:, c, at, :] for c in range(2) for r in refs], axis=0)


def middle_kernel(f_ref, back_ref, mid_ref, pump_ref, a_ref, w_ref, up_ref, down_ref, v_scratch, mid_scratch):
    f = wide(f_ref[...])
    pump = pump_ref[...]
    batch = 8

    def one(i, _):
        w = dot_wide(f, jnp.concatenate([gather_rows([a_ref], i * batch + j) for j in range(batch)], axis=1))
        for j in range(batch):
            wj = w[:, LANES * j : LANES * (j + 1)]
            re, im = kerr(wj[:FACTOR], wj[FACTOR:], pump)
            v = dot_wide(wide(back_ref[i * batch + j]), jnp.concatenate([re, im], axis=0))
            v_scratch[i * batch + j] = v.reshape(2, FACTOR, LANES)
        return 0

    lax.fori_loop(0, FACTOR // batch, one, 0)

    def two(i, _):
        for j in range(batch):
            o = i * batch + j
            v = dot_wide(wide(mid_ref[o]), gather_rows([v_scratch], o))
            mid_scratch[o] = v.reshape(2, FACTOR, LANES)
        return 0

    lax.fori_loop(0, FACTOR // batch, two, 0)

    eighth = w_ref.shape[2]
    size = batch // 2
    steps = eighth // size
    cut = LANES // 2

    def three(i, _):
        g, low = i // steps, (i % steps) * size
        s = [g * (2 * eighth) + h * eighth + low + j for h in range(2) for j in range(size)]
        w = dot_wide(f, jnp.concatenate([gather_rows([mid_scratch], at) for at in s], axis=1))
        for j in range(size):
            w0 = w[:, LANES * j : LANES * (j + 1)]
            w1 = w[:, LANES * (size + j) : LANES * (size + j + 1)]
            w_ref[g, 0, low + j] = w0.reshape(2, FACTOR, LANES)
            w_ref[g, 1, low + j] = w1.reshape(2, FACTOR, LANES)
            up = jnp.concatenate([w0[:, cut:], w1[:, cut:]], axis=1)
            down = jnp.concatenate([w0[:, :cut], w1[:, :cut]], axis=1)
            up_ref[g, low + j] = up.reshape(2, FACTOR, LANES)
            down_ref[g, low + j] = down.reshape(2, FACTOR, LANES)
        return 0

    lax.fori_loop(0, w_ref.shape[0] * steps, three, 0)


def last_kernel(tiles, w_ref, up_ref, down_ref, edge_ref, t_ref, te_ref, pump_ref, o_ref, up_buf, down_buf, stage, t_hi, t_lo, z_send, z_recv, x_send, x_recv):
    zz, yy, me = lax.axis_index("zz"), lax.axis_index("yy"), lax.axis_index("mode")
    groups, eighth = up_ref.shape[0], up_ref.shape[1]
    n = eighth * FACTOR
    cores = 2
    xs = groups // cores
    x, core = me // cores, me % cores
    has_before, has_after = zz > 0, zz < tiles - 1

    def group_at(k):
        return ((x + 1 + k // cores) % xs) * cores + (core + k + k // cores) % cores

    def peer(k, y):
        return {"yy": y, "mode": group_at(k)}

    barrier = pltpu.get_barrier_semaphore()

    def greet(where):
        pl.semaphore_signal(barrier, inc=1, device_id=where, device_id_type=MESH)

    for k in range(groups):
        greet(peer(k, 1 - yy))
        if k < groups - 1:
            greet(peer(k, yy))

    @pl.when(has_before)
    def _():
        greet({"zz": zz - 1})

    @pl.when(has_after)
    def _():
        greet({"zz": zz + 1})

    before = (zz + tiles - 1) // tiles
    after = 1 - (zz + 1) // tiles
    pl.semaphore_wait(barrier, 2 * groups - 1 + before + after)

    def upward(k):
        g = group_at(k)
        return pltpu.make_async_remote_copy(up_ref.at[g], up_buf.at[g], z_send.at[0, k], z_recv.at[0, k], device_id={"zz": zz + 1}, device_id_type=MESH)

    def downward(k):
        g = group_at(k)
        return pltpu.make_async_remote_copy(down_ref.at[g], down_buf.at[g], z_send.at[1, k], z_recv.at[1, k], device_id={"zz": zz - 1}, device_id_type=MESH)

    for k in range(groups):

        @pl.when(has_after)
        def _():
            upward(k).start()

        @pl.when(has_before)
        def _():
            downward(k).start()

    @pl.when(zz == 0)
    def _():
        up_buf[...] = jnp.zeros_like(up_buf)

    @pl.when(zz == tiles - 1)
    def _():
        down_buf[...] = jnp.zeros_like(down_buf)

    hi, lo = split(t_ref[...])
    t_hi[...] = hi
    t_lo[...] = lo
    mine = yy * groups + me

    def outward(k, y, at):
        return pltpu.make_async_remote_copy(stage.at[k, y], o_ref.at[mine], x_send.at[k, at], x_recv.at[k, at], device_id=peer(k, y), device_id_type=MESH)

    def one(k, _):
        g = group_at(k)

        @pl.when(has_before)
        def _():
            upward(k).wait_recv()

        @pl.when(has_after)
        def _():
            downward(k).wait_recv()

        parts = [w_ref[g, h, :, c].reshape(n, LANES) for h in range(2) for c in range(2)]
        parts += [ref[g, :, c].reshape(n, LANES) for ref in (up_buf, down_buf) for c in range(2)]
        y = dot3(jnp.concatenate(parts, axis=1), (t_hi[...], t_lo[...]))
        e = edge_ref[g].T
        for h in range(2):
            y = y + dot3(e[n * h : n * (h + 1)], te_ref[h])
        for side in range(2):
            re = y[:, LANES * side : LANES * (side + 1)]
            im = y[:, LANES * (2 + side) : LANES * (3 + side)]
            re, im = kerr(re, im, pump_ref[side : side + 1])
            stage[k, side, 0] = re
            stage[k, side, 1] = im
        outward(k, 1 - yy, 0).start()

        @pl.when(k < groups - 1)
        def _():
            outward(k, yy, 1).start()

        return 0

    lax.fori_loop(0, groups, one, 0)
    o_ref[mine] = stage[groups - 1, yy]
    for k in range(groups):
        outward(k, 1 - yy, 0).wait()
        if k < groups - 1:
            outward(k, yy, 1).wait()

        @pl.when(has_after)
        def _():
            upward(k).wait_send()

        @pl.when(has_before)
        def _():
            downward(k).wait_send()


def params():
    return pltpu.CompilerParams(vmem_limit_bytes=VMEM_LIMIT)


def whole(shape):
    return pl.BlockSpec(shape, lambda *_: (0,) * len(shape))


def body(tiles, groups, cycle_spectra, link_phase, pump_mask, detuning):
    modes, rows_in, cols = cycle_spectra.shape[1:]
    devices = 2 * groups
    width = cols // devices
    rows = 2 * rows_in
    half = modes // 2
    outer = modes // FACTOR
    zz = lax.axis_index("zz")
    block = lax.axis_index("yy") * groups + lax.axis_index("mode")
    up_perm = [(i, i + 1) for i in range(tiles - 1)]
    down_perm = [(i + 1, i) for i in range(tiles - 1)]

    def to_group(x):
        return lax.all_to_all(x, GROUP, split_axis=0, concat_axis=0, tiled=True)

    everyone = ("zz",) + GROUP
    cells = cycle_spectra.reshape(2, modes, rows_in, devices, width)
    none = jnp.zeros((2, modes, rows_in, 1, 2), F32)
    from_left = jnp.concatenate([none, cells[:, :, :, :-1, width - 2 :]], 3)
    from_right = jnp.concatenate([cells[:, :, :, 1:, :2], none], 3)
    rim = jnp.concatenate([from_left, from_right], 4).transpose(3, 0, 2, 4, 1)
    sites = jnp.concatenate([link_phase.astype(F32), detuning[None], pump_mask.astype(F32)[None]], 0)
    sites = jnp.pad(sites, ((0, 0), (0, 0), (2, 2)))
    sites = jnp.stack([sites[:, :, width * d : width * d + width + 4] for d in range(devices)])
    sites = jnp.pad(sites.reshape(devices, 4 * rows_in, width + 4), ((0, 0), (0, 0), (0, modes - width - 4)))
    edge_rows = 2 * rows_in * 4
    rim = jnp.concatenate([rim.reshape(devices, edge_rows, modes), sites], 1)
    rim = to_group(rim).reshape(2, groups, edge_rows + 4 * rows_in, modes)
    rim, cycle_spectra = lax.optimization_barrier((rim, cycle_spectra))
    packed = pl.pallas_call(
        pack_kernel,
        grid=(2,),
        in_specs=[pl.BlockSpec((1, 2, half, rows_in, cols), lambda c: (c, 0, 0, 0, 0))],
        out_specs=[pl.BlockSpec((devices, 1, half, LANES), lambda c: (0, c, 0, 0))],
        out_shape=[jax.ShapeDtypeStruct((devices, 2, half, LANES), F32)],
        compiler_params=params(),
    )(cycle_spectra.reshape(2, 2, half, rows_in, cols))[0]
    own = to_group(packed).reshape(2, groups, 2, half, LANES)
    rim_up = lax.ppermute(rim[1], "zz", up_perm)
    rim_down = lax.ppermute(rim[0], "zz", down_perm)
    kinds = [rim_up, rim[0], rim[1], rim_down]
    edge = jnp.concatenate([a[:, :edge_rows] for a in kinds], 1)
    ext = jnp.concatenate([a[0, edge_rows:, : width + 4].reshape(4, rows_in, width + 4) for a in kinds], 1)
    tr, ti = lattice_operator(ext, zz, block, tiles * rows, cols, rows, width)
    main, edge_op = operator_blocks(tr, ti, width)
    t_first = first_operator(main)
    t_last, edge_last = last_operator(main, edge_op)
    pump = PUMP_LEVEL * ext[3, 2 : 2 + rows, 2 : 2 + width]
    pump_flat = pump.reshape(1, rows * width)
    pump_half = pump.reshape(2, LANES // 2)
    pump_last = jnp.concatenate([pump_half, pump_half], 1)
    m_first, second, back, middle = mode_tables()
    up = lax.ppermute(own[1], "zz", up_perm)
    down = lax.ppermute(own[0], "zz", down_perm)

    full = (FACTOR, 2, FACTOR, LANES)
    stage = pl.pallas_call(
        first_kernel,
        grid=(groups,),
        in_specs=[
            pl.BlockSpec((2, 1, 2, half, LANES), lambda g: (0, g, 0, 0, 0)),
            pl.BlockSpec((1, 2, half, LANES), lambda g: (g, 0, 0, 0)),
            pl.BlockSpec((1, 2, half, LANES), lambda g: (g, 0, 0, 0)),
            pl.BlockSpec((1,) + edge.shape[1:], lambda g: (g, 0, 0)),
            whole(t_first.shape),
            whole(edge_op.shape),
            pl.BlockSpec((outer, LANES, LANES), lambda g: (g, 0, 0)),
        ],
        out_specs=pl.BlockSpec((outer, 2, FACTOR, LANES), lambda g: (g, 0, 0, 0)),
        out_shape=jax.ShapeDtypeStruct(full, F32),
        compiler_params=params(),
    )(own, up, down, edge, t_first, edge_op, m_first)

    eighth = outer // 2
    halo_shape = (groups, eighth, 2, FACTOR, LANES)
    wave, up, down = pl.pallas_call(
        middle_kernel,
        out_shape=[jax.ShapeDtypeStruct((groups, 2) + halo_shape[1:], F32)] + [jax.ShapeDtypeStruct(halo_shape, F32)] * 2,
        scratch_shapes=[pltpu.VMEM(full, F32), pltpu.VMEM(full, F32)],
        compiler_params=params(),
    )(second, back, middle, pump_flat, stage)

    rims = wave.reshape(FACTOR, 2, FACTOR, rows, width)
    sides = []
    for low, step in ((width - 2, 1), (0, -1)):
        cells = rims[..., low : low + 2].transpose(3, 1, 4, 0, 2).reshape(2, 2, 2, 2, M)
        took = []
        for source, turn in ((1, 1), (None, 0), (0, -1)):
            perm = []
            for at in range(tiles):
                for d in range(devices):
                    if 0 <= at + turn < tiles and 0 <= d + step < devices:
                        perm.append((at * devices + d, (at + turn) * devices + d + step))
            sent = cells if source is None else cells[source : source + 1]
            took.append(lax.ppermute(sent, everyone, perm))
        sides.append(jnp.concatenate(took, 0))
    edge = jnp.concatenate(sides, 3).transpose(0, 2, 1, 3, 4).reshape(-1, groups, modes).transpose(1, 0, 2)

    vmem = pl.BlockSpec(memory_space=pltpu.VMEM)
    arrived = pl.pallas_call(
        functools.partial(last_kernel, tiles),
        in_specs=[vmem] * 7,
        out_specs=vmem,
        out_shape=jax.ShapeDtypeStruct((devices, 2, half, LANES), F32),
        scratch_shapes=[
            pltpu.VMEM(halo_shape, F32),
            pltpu.VMEM(halo_shape, F32),
            pltpu.VMEM((groups, 2, 2, half, LANES), F32),
            pltpu.VMEM(t_last.shape, BF),
            pltpu.VMEM(t_last.shape, BF),
            pltpu.SemaphoreType.DMA((2, groups)),
            pltpu.SemaphoreType.DMA((2, groups)),
            pltpu.SemaphoreType.DMA((groups, 2)),
            pltpu.SemaphoreType.DMA((groups, 2)),
        ],
        compiler_params=pltpu.CompilerParams(vmem_limit_bytes=VMEM_LIMIT, collective_id=1, has_side_effects=True),
    )(wave, up, down, edge, t_last, edge_last, pump_last)
    samples = pl.pallas_call(
        unpack_kernel,
        grid=(2,),
        in_specs=[pl.BlockSpec((devices, 1, half, LANES), lambda c: (0, c, 0, 0))],
        out_specs=pl.BlockSpec((1, 2, half, rows_in, cols), lambda c: (c, 0, 0, 0, 0)),
        out_shape=jax.ShapeDtypeStruct((2, 2, half, rows_in, cols), F32),
        compiler_params=params(),
    )(arrived)
    return samples.reshape(2, modes, rows_in, cols)


def solution(mesh):
    names = mesh.axis_names
    tiles, groups = mesh.shape[names[0]], mesh.shape[names[1]]
    paired = Mesh(mesh.devices.reshape(tiles // 2, 2, groups), ("zz", "yy", "mode"))
    tile = ("zz", "yy")
    return jax.shard_map(
        functools.partial(body, tiles // 2, groups),
        mesh=paired,
        in_specs=(
            P(None, "mode", tile, None),
            P(None, tile, None),
            P(tile, None),
            P(tile, None),
        ),
        out_specs=P(None, "mode", tile, None),
        check_vma=False,
    )
```
